32 devices in a mesh: groups: 2 (over y), fsdp: 8 (over z, x), blk: 2 (over core).
Axes of the slice: x: 2, y: 2, z: 4, core: 2. Of those that a mesh axis runs over, the one named last changes fastest.
Arguments:
- block_input: bfloat16 [8192, 5120], P(('groups', 'fsdp', 'blk')), parts along dimension 0, may hold values from -3 to 3
- gate: float32 [10240], P('groups'), parts along dimension 0, may hold values from -6 to 6
- q_fresh: bfloat16 [8192, 2560], P(('groups', 'fsdp', 'blk')), parts along dimension 0, may hold values from -48.5 to 48.5
- kv_fresh: bfloat16 [8192, 2, 2560], P(('groups', 'fsdp', 'blk')), parts along dimension 0, may hold values from -6 to 6
- kv_cache: bfloat16 [8192, 2, 2560], P(('groups', 'fsdp', 'blk')), parts along dimension 0, may hold values from -6 to 6
- active_list: int32 [16, 2, 2], P(('groups', 'fsdp')), parts along dimension 0, may hold values from 0 to 1, as said below
- active_count: int32 [16, 2], P(('groups', 'fsdp')), parts along dimension 0, may hold values from 0 to 2, as said below
- key_list: int32 [16, 4, 3], P(('groups', 'fsdp')), parts along dimension 0, may hold values from 0 to 3, as said below
- out_weight: bfloat16 [2560, 5120], P('fsdp'), may hold values from -0.125 to 0.125
Outputs:
- block_output: bfloat16 [8192, 5120], P(('groups', 'fsdp', 'blk')), parts along dimension 0
The draws below stay inside these ranges and needn't reach their ends.
There are 2 independent parts, one for each index of `groups`. The reference program is written for one: setup_inputs(seed, part) draws one part's arguments, and reference() takes and returns one part's arrays. A program takes and returns all parts, laid end to end along the dimension named above; an argument that names none is the same for every part. Nothing has to cross between parts.
Inputs may be any that keep to these rules, and one draw needn't show every extreme that they name: `active_list`: each row [f, b] holds every tile number once; its first active_count[f, b] entries are the active tiles. `active_count`: some token block has all 2 tiles active. `key_list`: entry [f, g] holds 3 different tile ids of group f, the first one being g.
All inputs are finite; a program needn't handle non-finite values.
Results may differ from the reference program's by a relative error of at most 0.0034.
Values may be sent and summed in bfloat16 or wider, within the bound.
A program may use at most 128 MiB of HBM per device.

```python
import math
import jax
import jax.numpy as jnp
from jax import lax

D = 5120
HEADS = 20
HEAD_DIM = 128
TILE = 128
TILES_DEV = 2
HD = 2560
TOK_DEV = 256
GROUP_TILES = 4
KEY_TILES = 3
TOKENS = 4096
N_FSDP = 8
N_BLK = 2


def fresh_pair(key):
    base_key = jax.random.fold_in(key, 37)
    query_key, keys_key, values_key = jax.random.split(base_key, 3)
    queries = jnp.clip(2.0 * jax.random.normal(query_key, (TOKENS, HD), jnp.float32), -8.0, 8.0)
    key_rows = jnp.clip(jax.random.normal(keys_key, (TOKENS, HD), jnp.float32), -6.0, 6.0)
    value_rows = jnp.clip(jax.random.normal(values_key, (TOKENS, HD), jnp.float32), -6.0, 6.0)
    return (queries, jnp.stack([key_rows, value_rows], axis=1))


def draw_q_fresh(key, part):
    return fresh_pair(key)[0].astype(jnp.bfloat16)


def draw_kv_fresh(key, part):
    return fresh_pair(key)[1].astype(jnp.bfloat16)


def active_pair(key):
    base_key = jax.random.fold_in(key, 11)
    count_key, pick_key, order_key = jax.random.split(base_key, 3)
    block_count = N_FSDP * N_BLK
    counts = jax.random.randint(count_key, (block_count,), 0, TILES_DEV + 1)
    full_block = jax.random.randint(pick_key, (), 0, block_count)
    counts = jnp.where(jnp.arange(block_count, dtype=jnp.int32) == full_block, TILES_DEV, counts)
    ranking = jax.random.randint(order_key, (block_count, TILES_DEV), 0, 1 << 20) * TILES_DEV + jnp.arange(TILES_DEV, dtype=jnp.int32)[None, :]
    ordering = jnp.argsort(ranking, axis=1, stable=True).astype(jnp.int32)
    return (ordering.reshape(N_FSDP, N_BLK, TILES_DEV), counts.astype(jnp.int32).reshape(N_FSDP, N_BLK))


def draw_active_list(key, part):
    return active_pair(key)[0]


def draw_active_count(key, part):
    return active_pair(key)[1]


def draw_key_list(key, part):
    base_key = jax.random.fold_in(key, 23)
    tile_ids = jnp.arange(GROUP_TILES, dtype=jnp.int32)
    ranking = jax.random.randint(base_key, (N_FSDP, GROUP_TILES, GROUP_TILES), 0, 1 << 20) * GROUP_TILES + tile_ids[None, None, :]
    ranking = jnp.where(tile_ids[None, :, None] == tile_ids[None, None, :], -1, ranking)
    ordering = jnp.argsort(ranking, axis=2, stable=True).astype(jnp.int32)
    return ordering[:, :, :KEY_TILES]


def levels(rng, dims, cuts, low, top_value):
    level, own = 1.0, jax.random.fold_in(rng, 6)
    for dim, shards_of in cuts:
        draws = jnp.exp(jax.random.uniform(jax.random.fold_in(own, dim), (shards_of,), jnp.float32, low / len(cuts), top_value / len(cuts)))
        level = level * jnp.repeat(draws, dims[dim] // shards_of).reshape([-1 if axis == dim else 1 for axis in range(len(dims))])
    return level


def scatter_about(rng, shape, deviation, bound, shards=(), held_as=jnp.bfloat16):
    result = jax.random.normal(rng, shape, jnp.float32) * deviation
    if len(shards) > 0:
        result = levels(rng, shape, shards, -0.22, 0.18) * result
    return jnp.clip(result, min=-bound, max=bound).astype(held_as)


def setup_inputs(seed: int = 0, part: int = 0) -> dict:
    seeds = jax.random.split(jax.random.key(seed), 10)
    own_keys = jax.random.split(jax.random.fold_in(seeds[9], part), 10)
    return {
        "block_input": scatter_about(own_keys[0], (TOKENS, D), 0.5, 3.0, ((0, 16),)),
        "gate": scatter_about(own_keys[1], (D,), 1.5, 6.0, (), jnp.float32),
        "q_fresh": draw_q_fresh(jax.random.fold_in(jax.random.fold_in(seeds[9], part), 71), part),
        "kv_fresh": draw_kv_fresh(jax.random.fold_in(jax.random.fold_in(seeds[9], part), 71), part),
        "kv_cache": scatter_about(own_keys[4], (TOKENS, 2, HD), 1.0, 6.0, ((0, 16),)),
        "active_list": draw_active_list(jax.random.fold_in(jax.random.fold_in(seeds[9], part), 71), part),
        "active_count": draw_active_count(jax.random.fold_in(jax.random.fold_in(seeds[9], part), 71), part),
        "key_list": draw_key_list(jax.random.fold_in(jax.random.fold_in(seeds[9], part), 71), part),
        "out_weight": scatter_about(seeds[8], (HD, D), HD ** -0.5, 0.125, ((0, 8),)),
    }


MASKED = -1e+30

def block_partial(query_tile, key_rows, value_rows, allowed):
    tile_rows = query_tile.shape[0]
    query3 = query_tile.astype(jnp.float32).reshape(tile_rows, HEADS, HEAD_DIM)
    key3 = key_rows.astype(jnp.float32).reshape(key_rows.shape[0], HEADS, HEAD_DIM)
    value3 = value_rows.astype(jnp.float32).reshape(value_rows.shape[0], HEADS, HEAD_DIM)
    scores = jnp.einsum('qhd,khd->hqk', query3, key3) / math.sqrt(HEAD_DIM)
    scores = jnp.where(allowed[None, None, :], scores, MASKED)
    row_max = lax.optimization_barrier(jnp.max(scores, axis=2))
    exp_terms = jnp.where(allowed[None, None, :], jnp.exp(scores - row_max[:, :, None]), 0.0)
    row_total = lax.optimization_barrier(jnp.sum(exp_terms, axis=2))
    weights = lax.optimization_barrier(exp_terms.astype(jnp.bfloat16)).astype(jnp.float32)
    block_out = jnp.einsum('hqk,khd->hqd', weights, value3)
    return (block_out, row_max, row_total)

def reference(block_input, gate, q_fresh, kv_fresh, kv_cache, active_list, active_count, key_list, out_weight):
    block_count = N_FSDP * N_BLK
    slot_ids = jnp.arange(TILES_DEV, dtype=jnp.int32)
    tile_lists = active_list.reshape(block_count, TILES_DEV)
    tile_counts = active_count.reshape(block_count)
    listed = (tile_lists[:, :, None] == slot_ids[None, None, :]) & (slot_ids[None, :, None] < tile_counts[:, None, None])
    tile_active = jnp.any(listed, axis=1).reshape(block_count * TILES_DEV)
    row_active = jnp.repeat(tile_active, TILE)
    resident = jnp.where(row_active[:, None, None], kv_fresh, kv_cache)

    def one_tile(tile_index):
        group_id = tile_index // GROUP_TILES
        group_tile = tile_index % GROUP_TILES
        row_start = tile_index * TILE
        input_tile = lax.dynamic_slice_in_dim(block_input, row_start, TILE, 0)

        def compute_tile():
            query_tile = lax.dynamic_slice_in_dim(q_fresh, row_start, TILE, 0)
            listed_keys = key_list[group_id, group_tile]
            partials = []
            for key_side in range(N_BLK):
                row_base = (group_id * N_BLK + key_side) * TOK_DEV
                block_kv = lax.dynamic_slice_in_dim(resident, row_base, TOK_DEV, 0)
                key_tiles = key_side * TILES_DEV + slot_ids
                allowed_tiles = jnp.any(key_tiles[:, None] == listed_keys[None, :], axis=1)
                allowed = jnp.repeat(allowed_tiles, TILE)
                partials.append(block_partial(query_tile, block_kv[:, 0], block_kv[:, 1], allowed))
            joint_max = jnp.maximum(partials[0][1], partials[1][1])
            scale_zero = jnp.exp(partials[0][1] - joint_max)
            scale_one = jnp.exp(partials[1][1] - joint_max)
            summed = partials[0][0] * scale_zero[:, :, None] + partials[1][0] * scale_one[:, :, None]
            denom = partials[0][2] * scale_zero + partials[1][2] * scale_one
            attended = (summed / denom[:, :, None]).transpose(1, 0, 2).reshape(TILE, HD).astype(jnp.bfloat16)
            projected = jnp.dot(attended, out_weight, preferred_element_type=jnp.float32)
            return (input_tile.astype(jnp.float32) + gate[None, :] * projected).astype(jnp.bfloat16)

        def skip_tile():
            return input_tile
        return lax.cond(tile_active[tile_index], compute_tile, skip_tile)
    tiles = lax.map(one_tile, jnp.arange(TOKENS // TILE, dtype=jnp.int32))
    return tiles.reshape(TOKENS, D)
```

```python
import functools
import math

import jax
import jax.numpy as jnp
from jax import lax
from jax.experimental import pallas as pl
from jax.experimental.pallas import tpu as pltpu
from jax.sharding import PartitionSpec as P

HEADS = 20
HEAD_DIM = 128


MASKED = -1e30


def swapped(block, axis, apart):
    count = lax.axis_size(axis)
    route = []
    for low in range(count):
        high = low | 1 << apart
        if high != low and high < count:
            route += [(low, high), (high, low)]
    return lax.ppermute(block, axis, route)


def tile_flags(tile_list, tile_count):
    slot_ids = jnp.arange(tile_list.shape[0], dtype=jnp.int32)
    listed = (tile_list[:, None] == slot_ids[None, :]) & (slot_ids[:, None] < tile_count)
    return jnp.any(listed, axis=0)


def block_partial(query_tile, key_rows, value_rows, allowed):
    tile_rows = query_tile.shape[0]
    query3 = query_tile.reshape(tile_rows, HEADS, HEAD_DIM)
    key3 = key_rows.reshape(key_rows.shape[0], HEADS, HEAD_DIM)
    value3 = value_rows.reshape(value_rows.shape[0], HEADS, HEAD_DIM)
    scores = jnp.einsum(
        "qhd,khd->hqk", query3, key3, preferred_element_type=jnp.float32
    ) / math.sqrt(HEAD_DIM)
    scores = jnp.where(allowed[None, None, :], scores, MASKED)
    row_max = jnp.max(scores, axis=2)
    exp_terms = jnp.where(allowed[None, None, :], jnp.exp(scores - row_max[:, :, None]), 0.0)
    row_total = jnp.sum(exp_terms, axis=2)
    weights = exp_terms.astype(jnp.bfloat16)
    block_out = jnp.einsum("hqk,khd->hqd", weights, value3, preferred_element_type=jnp.float32)
    return (block_out, row_max, row_total)


def attend_block(
    queries, tile_list, tile_count, query_side, key_rows, value_rows, key_side, key_table
):
    tiles_dev = tile_list.shape[0]
    tile_rows = queries.shape[0] // tiles_dev
    slot_ids = jnp.arange(tiles_dev, dtype=jnp.int32)
    key_tiles = key_side * tiles_dev + slot_ids
    init_state = (
        jnp.zeros((tiles_dev, HEADS, tile_rows, HEAD_DIM), jnp.float32),
        jnp.full((tiles_dev, HEADS, tile_rows), MASKED, jnp.float32),
        jnp.zeros((tiles_dev, HEADS, tile_rows), jnp.float32),
    )

    def one_slot(slot_idx, carry_state):
        tile_pos = tile_list[slot_idx]
        query_tile = lax.dynamic_slice_in_dim(queries, tile_pos * tile_rows, tile_rows, 0)
        listed = key_table[query_side * tiles_dev + tile_pos]
        allowed_tiles = jnp.any(key_tiles[:, None] == listed[None, :], axis=1)
        allowed = jnp.repeat(allowed_tiles, tile_rows, total_repeat_length=tiles_dev * tile_rows)
        partial_value = block_partial(query_tile, key_rows, value_rows, allowed)
        return tuple(
            (whole.at[tile_pos].set(piece) for whole, piece in zip(carry_state, partial_value))
        )

    return lax.fori_loop(0, tile_count, one_slot, init_state)


def merge_states(earlier, later_state):
    out_one, max_one, total_one = earlier
    out_two, max_two, total_two = later_state
    joint_max = jnp.maximum(max_one, max_two)
    scale_one = jnp.exp(max_one - joint_max)
    scale_two = jnp.exp(max_two - joint_max)
    summed = out_one * scale_one[..., None] + out_two * scale_two[..., None]
    return (summed, total_one * scale_one + total_two * scale_two)


def local(
    block_input, gate, q_fresh, kv_fresh, kv_cache, active_list, active_count, key_list, out_weight
):
    own_side = lax.axis_index("blk")
    other_side = 1 - own_side
    tiles_dev = active_list.shape[2]
    tok_dev = block_input.shape[0]
    tile_rows = tok_dev // tiles_dev
    own_list = active_list[0, own_side]
    own_count = active_count[0, own_side]
    flags = tile_flags(own_list, own_count)
    row_flags = jnp.repeat(flags, tile_rows, total_repeat_length=tok_dev)
    resident = jnp.where(row_flags[:, None, None], kv_fresh, kv_cache)
    key_table = key_list[0]
    own_state = attend_block(
        q_fresh, own_list, own_count, own_side, resident[:, 0], resident[:, 1], own_side, key_table
    )
    other_kv = swapped(resident, "blk", 0)
    other_state = attend_block(
        q_fresh,
        own_list,
        own_count,
        own_side,
        other_kv[:, 0],
        other_kv[:, 1],
        other_side,
        key_table,
    )
    summed, denom = merge_states(own_state, other_state)
    denom = jnp.where(flags[:, None, None], denom, 1.0)
    attended = (
        (summed / denom[..., None])
        .transpose(0, 2, 1, 3)
        .reshape(tok_dev, HEADS * HEAD_DIM)
        .astype(jnp.bfloat16)
    )
    half_cols = out_weight.shape[1] // 2
    own_cols = lax.dynamic_slice_in_dim(out_weight, own_side * half_cols, half_cols, 1)
    half_weight = lax.all_gather(own_cols, "fsdp", axis=0, tiled=True)
    partner_rows = swapped(attended, "blk", 0)
    own_part = jnp.dot(attended, half_weight, preferred_element_type=jnp.float32)
    partner_part = jnp.dot(partner_rows, half_weight, preferred_element_type=jnp.float32)
    returned = swapped(partner_part, "blk", 0)
    projected = jnp.where(
        own_side == 0,
        jnp.concatenate([own_part, returned], axis=1),
        jnp.concatenate([returned, own_part], axis=1),
    )
    mixed = block_input.astype(jnp.float32) + gate[None, :] * projected
    return jnp.where(row_flags[:, None], mixed.astype(jnp.bfloat16), block_input)


MESH = pl.DeviceIdType.MESH
LINE = 2
LONG = 4
SHORT = 2
UNITS = 2 * LONG + SHORT
PACK = 2
GROUPED = 4


def fused(
    depth,
    active_list,
    active_count,
    key_list,
    block_hbm,
    gate_ref,
    q_hbm,
    fresh_hbm,
    cache_hbm,
    w_hbm,
    out_ref,
    w_long,
    w_short,
    queries,
    fresh,
    cache,
    wide,
    keys,
    values,
    attended,
    mixed_in,
    pair_in,
    pair_out,
    sent,
    received,
    load_sem,
    own_sem,
    w_send,
    w_recv,
    kv_send,
    kv_recv,
    in_send,
    in_recv,
    a_send,
    a_recv,
    p_send,
    p_recv,
    out_send,
    out_recv,
):
    me = lax.axis_index("fsdp")
    z, x = me // LINE, me % LINE
    y = lax.axis_index("groups")
    b = lax.axis_index("blk")
    rows = w_hbm.shape[0]
    tok = q_hbm.shape[0]
    quarter = w_hbm.shape[1] // 4
    unit = quarter // UNITS
    tiles = active_list.shape[2]
    tile_rows = tok // tiles
    heads = q_hbm.shape[1] // HEAD_DIM
    sets = heads // GROUPED
    piece = PACK * HEAD_DIM
    pieces = heads // PACK
    listed = key_list.shape[0]

    def quarter_of(group, core):
        return pl.multiple_of((2 * group + core) * quarter, 128)

    mine = quarter_of(y, b)

    barrier = pltpu.get_barrier_semaphore()
    targets = (
        (z < depth - 1, {"fsdp": me + LINE}),
        (z > 0, {"fsdp": me - LINE}),
        (None, {"fsdp": z * LINE + 1 - x}),
    )
    twin = {"groups": 1 - y}
    core = {"blk": 1 - b}
    cross = {"groups": 1 - y, "blk": 1 - b}

    def when(cond, body):
        if cond is None:
            body()
        else:
            pl.when(cond)(body)

    def greet(device):
        pl.semaphore_signal(barrier, inc=1, device_id=device, device_id_type=MESH)

    for cond, device in targets + ((None, twin), (None, core), (None, cross)):
        when(cond, functools.partial(greet, device))

    def remote(src, dst, send, recv, device):
        return pltpu.make_async_remote_copy(
            src_ref=src,
            dst_ref=dst,
            send_sem=send,
            recv_sem=recv,
            device_id=device,
            device_id_type=MESH,
        )

    def extent(k):
        return (2 * k * unit, 2 * unit) if k < LONG else ((LONG + k) * unit, unit)

    def weight(k):
        return w_long.at[k] if k < LONG else w_short.at[k - LONG]

    def shard(k, s):
        return weight(k).at[pl.ds(pl.multiple_of(s * rows, 16), rows), :]

    def own_cols(k):
        low, size = extent(k)
        return w_hbm.at[:, pl.ds(pl.multiple_of(mine + low, 128), size)]

    streams = range(LONG + SHORT)

    loads = [
        pltpu.make_async_copy(fresh_hbm, fresh, load_sem.at[0]),
        pltpu.make_async_copy(cache_hbm, cache, load_sem.at[1]),
        pltpu.make_async_copy(q_hbm, queries, load_sem.at[2]),
        pltpu.make_async_copy(block_hbm, mixed_in, load_sem.at[3]),
    ]
    owns = [pltpu.make_async_copy(own_cols(k), shard(k, me), own_sem.at[k]) for k in streams]
    for load in loads[:3]:
        load.start()

    pl.semaphore_wait(barrier, 4 + (z > 0).astype(jnp.int32) + (z < depth - 1).astype(jnp.int32))

    swap_in = remote(
        block_hbm.at[:, pl.ds(quarter_of(y, 1 - b), quarter)],
        pair_in,
        in_send.at[0],
        in_recv.at[0],
        core,
    )

    def shard_copy(k, s, way, own=False):
        return remote(
            own_cols(k) if own else shard(k, s),
            shard(k, s),
            w_send.at[k, s, way],
            w_recv.at[k, s],
            targets[way][1],
        )

    def ways_of(k, dz, dx):
        if k < LONG and dx == 1:
            return []
        found = []
        if dz <= 0:
            found.append(0)
        if dz >= 0:
            found.append(1)
        if k < LONG or (dz, dx) == (0, 0):
            found.append(2)
        return found

    def inside(dz, body):
        if dz < 0:
            pl.when(z + dz >= 0)(body)
        elif dz > 0:
            pl.when(z + dz < depth)(body)
        else:
            body()

    def visit(k, dz, dx, done=False):
        s = (z + dz) * LINE + (x if dx == 0 else 1 - x)
        own = (dz, dx) == (0, 0)

        def body():
            if not done and not own:
                shard_copy(k, s, 2).wait_recv()

            def act(way):
                copy = shard_copy(k, s, way, own)
                if done:
                    copy.wait_send()
                else:
                    copy.start()

            for way in ways_of(k, dz, dx):
                when(targets[way][0], functools.partial(act, way))

        inside(dz, body)

    def launch(*which):
        for k in which:
            visit(k, 0, 0)

    def relay(k, far):
        for dz in (-far, far):
            visit(k, dz, 0)
            if k >= LONG:
                visit(k, dz, 1)

    def side(k):
        visit(k, 0, 1)

    def settle_long(k):
        visit(k, 0, 1)
        for far in range(1, depth):
            visit(k, -far, 1)
            visit(k, far, 1)

    launch(0, 1, 2)

    def is_active(core_side, a):
        found = jnp.int32(0)
        for slot in range(tiles):
            hit = (active_list[0, core_side, slot] == a) & (slot < active_count[0, core_side])
            found = jnp.where(hit, jnp.int32(1), found)
        return found

    flags = [[is_active(core_side, a) for a in range(tiles)] for core_side in (b, 1 - b)]

    whole = pl.ds(pl.multiple_of(b * tok, 16), tok)

    def split_pair(g, i):
        for k in range(PACK):
            local_col = pl.multiple_of((i * PACK + k) * HEAD_DIM, 128)
            local_cols = pl.ds(local_col, HEAD_DIM)
            cols = pl.ds(pl.multiple_of(g * GROUPED * HEAD_DIM + local_col, 128), HEAD_DIM)
            for a in range(tiles):
                span = pl.ds(a * tile_rows, tile_rows)
                pair = jnp.where(flags[0][a] > 0, fresh[span, :, cols], cache[span, :, cols])
                pair = pair.reshape(2 * tile_rows, HEAD_DIM)
                wide[k, pl.ds(2 * a * tile_rows, 2 * tile_rows), :] = pair.astype(jnp.float32)
            keys[g][whole, local_cols] = wide[k, pl.ds(0, tok, 2), :].astype(jnp.bfloat16)
            values[g][whole, local_cols] = wide[k, pl.ds(1, tok, 2), :].astype(jnp.bfloat16)

    def kv_swap(g):
        return [
            remote(
                ref.at[whole, :], ref.at[whole, :], kv_send.at[j, g], kv_recv.at[j, g], core
            )
            for j, ref in enumerate((keys[g], values[g]))
        ]

    for load in loads[:2]:
        load.wait()
    for g in range(sets):
        pl.loop(0, GROUPED // PACK)(functools.partial(split_pair, g))
        for copy in kv_swap(g):
            copy.start()
    loads[2].wait()

    def is_listed(a, tile):
        found = jnp.int32(0)
        for t in range(listed):
            found = jnp.where(key_list[t, 0, b * tiles + a] == tile, jnp.int32(1), found)
        return found

    def tile_span(core_side, a):
        return pl.ds(pl.multiple_of(core_side * tok + a * tile_rows, 16), tile_rows)

    first_far, last_far = tile_span(1 - b, 0), tile_span(1 - b, 1)
    use_near = [is_listed(a, b * tiles + 1 - a) for a in range(tiles)]
    use_last = [is_listed(a, (1 - b) * tiles + 1) for a in range(tiles)]

    def three_tiles(ref, cols, a):
        spare = ref[first_far, cols]
        second = jnp.where(use_near[a] > 0, ref[tile_span(b, 1 - a), cols], spare)
        third = jnp.where(use_last[a] > 0, ref[last_far, cols], spare)
        return jnp.concatenate([ref[tile_span(b, a), cols], second, third], axis=0)

    factor = math.log2(math.e) / math.sqrt(HEAD_DIM)

    def rows_of(slot):
        return pl.ds(slot * tok, tok)

    def a_copies(n):
        cols = pl.ds(pl.multiple_of(n * piece, 128), piece)
        own = attended.at[rows_of(0), cols]
        over = attended.at[rows_of(2), cols]
        return (
            remote(own, over, a_send.at[0, n], a_recv.at[0, n], twin),
            remote(own, attended.at[rows_of(1), cols], a_send.at[1, n], a_recv.at[1, n], core),
            remote(over, attended.at[rows_of(3), cols], a_send.at[2, n], a_recv.at[2, n], core),
        )

    def attend(g, i):
        for k in range(PACK):
            local_col = pl.multiple_of((i * PACK + k) * HEAD_DIM, 128)
            local_cols = pl.ds(local_col, HEAD_DIM)
            cols = pl.ds(pl.multiple_of(g * GROUPED * HEAD_DIM + local_col, 128), HEAD_DIM)
            for a in range(tiles):
                query = queries[pl.ds(a * tile_rows, tile_rows), cols]
                key_rows = three_tiles(keys[g], local_cols, a)
                value_rows = three_tiles(values[g], local_cols, a)
                scores = lax.dot_general(
                    query, key_rows, (((1,), (1,)), ((), ())), preferred_element_type=jnp.float32
                )
                top = jnp.max(scores, axis=1, keepdims=True)
                terms = jnp.exp2((scores - top) * factor)
                total = jnp.sum(terms, axis=1, keepdims=True)
                summed = jnp.dot(
                    terms.astype(jnp.bfloat16), value_rows, preferred_element_type=jnp.float32
                )
                attended[pl.ds(a * tile_rows, tile_rows), cols] = (summed / total).astype(
                    jnp.bfloat16
                )
        n = g * (GROUPED // PACK) + i
        over, beside, _ = a_copies(n)
        over.start()
        beside.start()

    def attend_set(g):
        for copy in kv_swap(g):
            copy.wait_recv()
        pl.loop(0, GROUPED // PACK)(functools.partial(attend, g))

    def pass_on(low, high):
        @pl.loop(low, high)
        def _(n):
            over, _, onward = a_copies(n)
            over.wait_recv()
            onward.start()

    def p_copies(k):
        low, size = extent(k)
        cols = pl.ds(low, size)
        return [
            remote(
                sent.at[pl.ds(j * tok, tok), cols],
                received.at[pl.ds(j * tok, tok), cols],
                p_send.at[k, j],
                p_recv.at[k, j],
                device,
            )
            for j, device in enumerate((twin, cross))
        ]

    def out_copy(k):
        low, size = extent(k)
        return remote(
            pair_out.at[:, pl.ds(low, size)],
            out_ref.at[:, pl.ds(pl.multiple_of(mine + low, 128), size)],
            out_send.at[k],
            out_recv.at[k],
            core,
        )

    def far_part(k):
        low, size = extent(k)
        for j in range(2):
            part = jnp.dot(
                attended[rows_of(2 + j), :], weight(k)[...], preferred_element_type=jnp.float32
            )
            sent[pl.ds(j * tok, tok), pl.ds(low, size)] = part.astype(jnp.bfloat16)
            p_copies(k)[j].start()

    def blend(before, gate, part, flag):
        before = before.astype(jnp.float32)
        return jnp.where(flag > 0, before + gate * part, before).astype(jnp.bfloat16)

    def near_part(k):
        low, size = extent(k)
        cols = pl.ds(pl.multiple_of(mine + low, 128), size)
        gate = gate_ref[:, cols]
        part = jnp.dot(attended[rows_of(1), :], weight(k)[...], preferred_element_type=jnp.float32)
        for a in range(tiles):
            span = pl.ds(a * tile_rows, tile_rows)
            pair_out[span, pl.ds(low, size)] = blend(
                pair_in[span, pl.ds(low, size)],
                gate,
                part[a * tile_rows : (a + 1) * tile_rows],
                flags[1][a],
            )
        out_copy(k).start()
        part = jnp.dot(attended[rows_of(0), :], weight(k)[...], preferred_element_type=jnp.float32)
        for a in range(tiles):
            span = pl.ds(a * tile_rows, tile_rows)
            out_ref[span, cols] = blend(
                mixed_in[span, cols], gate, part[a * tile_rows : (a + 1) * tile_rows], flags[0][a]
            )

    def take(k):
        low, size = extent(k)
        for j, copy in enumerate(p_copies(k)):
            copy.wait_recv()
            base = quarter_of(1 - y, b if j == 0 else 1 - b)
            cols = pl.ds(pl.multiple_of(base + low, 128), size)
            gate = gate_ref[:, cols]
            for a in range(tiles):
                span = pl.ds(a * tile_rows, tile_rows)
                part = received[pl.ds(j * tok + a * tile_rows, tile_rows), pl.ds(low, size)]
                out_ref[span, cols] = blend(
                    mixed_in[span, cols], gate, part.astype(jnp.float32), flags[0][a]
                )

    for own in owns:
        own.start()
    loads[3].start()
    swap_in.start()

    relay(0, 1)
    relay(1, 1)
    attend_set(0)
    attend_set(1)
    relay(2, 1)
    relay(0, 2)
    attend_set(2)
    relay(1, 2)
    attend_set(3)
    launch(4, 5)
    relay(0, 3)
    attend_set(4)
    relay(1, 3)
    relay(2, 2)
    relay(2, 3)
    pass_on(0, 5)
    launch(3)
    relay(3, 1)
    side(4)
    side(5)
    relay(3, 2)
    relay(3, 3)
    pass_on(5, 10)

    @pl.loop(0, pieces)
    def _(n):
        _, beside, onward = a_copies(n)
        beside.wait_recv()
        onward.wait_recv()

    loads[3].wait()
    swap_in.wait_recv()
    for k in range(LONG):
        settle_long(k)
        owns[k].wait()
        far_part(k)
        if k == 0:
            relay(4, 1)
            relay(5, 1)
        if k == 1:
            relay(4, 2)
            relay(5, 2)
        near_part(k)
        if k >= 1:
            take(k - 1)
    for k in range(LONG, LONG + SHORT):
        relay(k, 3)
        owns[k].wait()
        far_part(k)
    for k in range(LONG, LONG + SHORT):
        near_part(k)
        take(k - 1)
    take(LONG + SHORT - 1)

    swap_in.wait_send()
    for g in range(sets):
        for copy in kv_swap(g):
            copy.wait_send()

    @pl.loop(0, pieces)
    def _(n):
        for copy in a_copies(n):
            copy.wait_send()

    for k in streams:
        visit(k, 0, 0, done=True)
        if k >= LONG:
            visit(k, 0, 1, done=True)
        for far in range(1, depth):
            for dz in (-far, far):
                for dx in range(LINE if k >= LONG else 1):
                    visit(k, dz, dx, done=True)
        for copy in p_copies(k):
            copy.wait_send()
        out_copy(k).wait()


def local_fused(
    count,
    block_input, gate, q_fresh, kv_fresh, kv_cache, active_list, active_count, key_list, out_weight
):
    tok, width = block_input.shape
    rows = out_weight.shape[0]
    quarter = width // 4
    unit = quarter // UNITS
    columns = q_fresh.shape[1]
    heads = columns // HEAD_DIM
    sets = heads // GROUPED
    pieces = heads // PACK
    streams = LONG + SHORT
    smem = pl.BlockSpec(memory_space=pltpu.SMEM)
    anywhere = pl.BlockSpec(memory_space=pltpu.HBM)
    dma = pltpu.SemaphoreType.DMA

    def vmem(*shape):
        return pltpu.VMEM(shape, jnp.bfloat16)

    return pl.pallas_call(
        functools.partial(fused, count // LINE),
        out_shape=pltpu.VMEM((tok, width), jnp.bfloat16),
        in_specs=[smem] * 3
        + [anywhere, pl.BlockSpec(memory_space=pltpu.VMEM)]
        + [anywhere] * 4,
        out_specs=pl.BlockSpec(memory_space=pltpu.VMEM),
        scratch_shapes=[
            vmem(LONG, count * rows, 2 * unit),
            vmem(SHORT, count * rows, unit),
            vmem(tok, columns),
            vmem(tok, 2, columns),
            vmem(tok, 2, columns),
            pltpu.VMEM((PACK, 2 * tok, HEAD_DIM), jnp.float32),
            [vmem(2 * tok, GROUPED * HEAD_DIM) for _ in range(sets)],
            [vmem(2 * tok, GROUPED * HEAD_DIM) for _ in range(sets)],
            vmem(4 * tok, columns),
            vmem(tok, width),
            vmem(tok, quarter),
            vmem(tok, quarter),
            vmem(2 * tok, quarter),
            vmem(2 * tok, quarter),
            dma((4,)),
            dma((streams,)),
            dma((streams, count, 3)),
            dma((streams, count)),
            dma((2, sets)),
            dma((2, sets)),
            dma((1,)),
            dma((1,)),
            dma((3, pieces)),
            dma((3, pieces)),
            dma((streams, 2)),
            dma((streams, 2)),
            dma((streams,)),
            dma((streams,)),
        ],
        compiler_params=pltpu.CompilerParams(
            collective_id=0, has_side_effects=True, vmem_limit_bytes=56000000
        ),
    )(
        active_list,
        active_count,
        key_list.transpose(2, 0, 1),
        block_input,
        gate[None, :],
        q_fresh,
        kv_fresh,
        kv_cache,
        out_weight,
    )


def per_device(groups, count, cores, *args):
    rows, width = args[-1].shape
    columns = args[2].shape[1]
    fits = groups == 2 and cores == 2 and count % LINE == 0 and rows % 16 == 0
    fits = fits and width % (4 * UNITS * 128) == 0 and count * rows * width < 1 << 24
    fits = fits and columns % (GROUPED * HEAD_DIM) == 0
    fits = fits and args[5].shape[2] == 2 and args[7].shape[1:] == (4, 3)
    return local_fused(count, *args) if fits else local(*args)


def solution(mesh):
    in_specs = (
        P(("groups", "fsdp", "blk"), None),
        P("groups"),
        P(("groups", "fsdp", "blk"), None),
        P(("groups", "fsdp", "blk"), None, None),
        P(("groups", "fsdp", "blk"), None, None),
        P(("groups", "fsdp"), None, None),
        P(("groups", "fsdp"), None),
        P(("groups", "fsdp"), None, None),
        P("fsdp", None),
    )
    sizes = [mesh.shape[axis] for axis in ("groups", "fsdp", "blk")]
    body = functools.partial(per_device, *sizes)
    out_specs = P(("groups", "fsdp", "blk"), None)
    return jax.shard_map(body, mesh=mesh, in_specs=in_specs, out_specs=out_specs, check_vma=False)
```

```python
import functools
import math

import jax
import jax.numpy as jnp
from jax import lax
from jax.experimental import pallas as pl
from jax.experimental.pallas import tpu as pltpu
from jax.sharding import PartitionSpec as P

HEADS = 20
HEAD_DIM = 128


MASKED = -1e30


def swapped(block, axis, apart):
    count = lax.axis_size(axis)
    route = []
    for low in range(count):
        high = low | 1 << apart
        if high != low and high < count:
            route += [(low, high), (high, low)]
    return lax.ppermute(block, axis, route)


def tile_flags(tile_list, tile_count):
    slot_ids = jnp.arange(tile_list.shape[0], dtype=jnp.int32)
    listed = (tile_list[:, None] == slot_ids[None, :]) & (slot_ids[:, None] < tile_count)
    return jnp.any(listed, axis=0)


def block_partial(query_tile, key_rows, value_rows, allowed):
    tile_rows = query_tile.shape[0]
    query3 = query_tile.reshape(tile_rows, HEADS, HEAD_DIM)
    key3 = key_rows.reshape(key_rows.shape[0], HEADS, HEAD_DIM)
    value3 = value_rows.reshape(value_rows.shape[0], HEADS, HEAD_DIM)
    scores = jnp.einsum(
        "qhd,khd->hqk", query3, key3, preferred_element_type=jnp.float32
    ) / math.sqrt(HEAD_DIM)
    scores = jnp.where(allowed[None, None, :], scores, MASKED)
    row_max = jnp.max(scores, axis=2)
    exp_terms = jnp.where(allowed[None, None, :], jnp.exp(scores - row_max[:, :, None]), 0.0)
    row_total = jnp.sum(exp_terms, axis=2)
    weights = exp_terms.astype(jnp.bfloat16)
    block_out = jnp.einsum("hqk,khd->hqd", weights, value3, preferred_element_type=jnp.float32)
    return (block_out, row_max, row_total)


def attend_block(
    queries, tile_list, tile_count, query_side, key_rows, value_rows, key_side, key_table
):
    tiles_dev = tile_list.shape[0]
    tile_rows = queries.shape[0] // tiles_dev
    slot_ids = jnp.arange(tiles_dev, dtype=jnp.int32)
    key_tiles = key_side * tiles_dev + slot_ids
    init_state = (
        jnp.zeros((tiles_dev, HEADS, tile_rows, HEAD_DIM), jnp.float32),
        jnp.full((tiles_dev, HEADS, tile_rows), MASKED, jnp.float32),
        jnp.zeros((tiles_dev, HEADS, tile_rows), jnp.float32),
    )

    def one_slot(slot_idx, carry_state):
        tile_pos = tile_list[slot_idx]
        query_tile = lax.dynamic_slice_in_dim(queries, tile_pos * tile_rows, tile_rows, 0)
        listed = key_table[query_side * tiles_dev + tile_pos]
        allowed_tiles = jnp.any(key_tiles[:, None] == listed[None, :], axis=1)
        allowed = jnp.repeat(allowed_tiles, tile_rows, total_repeat_length=tiles_dev * tile_rows)
        partial_value = block_partial(query_tile, key_rows, value_rows, allowed)
        return tuple(
            (whole.at[tile_pos].set(piece) for whole, piece in zip(carry_state, partial_value))
        )

    return lax.fori_loop(0, tile_count, one_slot, init_state)


def merge_states(earlier, later_state):
    out_one, max_one, total_one = earlier
    out_two, max_two, total_two = later_state
    joint_max = jnp.maximum(max_one, max_two)
    scale_one = jnp.exp(max_one - joint_max)
    scale_two = jnp.exp(max_two - joint_max)
    summed = out_one * scale_one[..., None] + out_two * scale_two[..., None]
    return (summed, total_one * scale_one + total_two * scale_two)


def local(
    block_input, gate, q_fresh, kv_fresh, kv_cache, active_list, active_count, key_list, out_weight
):
    own_side = lax.axis_index("blk")
    other_side = 1 - own_side
    tiles_dev = active_list.shape[2]
    tok_dev = block_input.shape[0]
    tile_rows = tok_dev // tiles_dev
    own_list = active_list[0, own_side]
    own_count = active_count[0, own_side]
    flags = tile_flags(own_list, own_count)
    row_flags = jnp.repeat(flags, tile_rows, total_repeat_length=tok_dev)
    resident = jnp.where(row_flags[:, None, None], kv_fresh, kv_cache)
    key_table = key_list[0]
    own_state = attend_block(
        q_fresh, own_list, own_count, own_side, resident[:, 0], resident[:, 1], own_side, key_table
    )
    other_kv = swapped(resident, "blk", 0)
    other_state = attend_block(
        q_fresh,
        own_list,
        own_count,
        own_side,
        other_kv[:, 0],
        other_kv[:, 1],
        other_side,
        key_table,
    )
    summed, denom = merge_states(own_state, other_state)
    denom = jnp.where(flags[:, None, None], denom, 1.0)
    attended = (
        (summed / denom[..., None])
        .transpose(0, 2, 1, 3)
        .reshape(tok_dev, HEADS * HEAD_DIM)
        .astype(jnp.bfloat16)
    )
    half_cols = out_weight.shape[1] // 2
    own_cols = lax.dynamic_slice_in_dim(out_weight, own_side * half_cols, half_cols, 1)
    half_weight = lax.all_gather(own_cols, "fsdp", axis=0, tiled=True)
    partner_rows = swapped(attended, "blk", 0)
    own_part = jnp.dot(attended, half_weight, preferred_element_type=jnp.float32)
    partner_part = jnp.dot(partner_rows, half_weight, preferred_element_type=jnp.float32)
    returned = swapped(partner_part, "blk", 0)
    projected = jnp.where(
        own_side == 0,
        jnp.concatenate([own_part, returned], axis=1),
        jnp.concatenate([returned, own_part], axis=1),
    )
    mixed = block_input.astype(jnp.float32) + gate[None, :] * projected
    return jnp.where(row_flags[:, None], mixed.astype(jnp.bfloat16), block_input)


MESH = pl.DeviceIdType.MESH
LINE = 2
LONG = 4
SHORT = 2
UNITS = 2 * LONG + SHORT
PACK = 2
GROUPED = 4
ORDER = (
    ("launch", 4), ("launch", 1), ("launch", 5), ("launch", 0), ("launch", 2), ("settle",),
    ("relay", 1, -1), ("attend", 0), ("relay", 1, 1), ("attend", 1), ("relay", 0, 1),
    ("forward", 0), ("side", 4), ("relay", 2, -1), ("attend", 2), ("relay", 0, -1),
    ("relay", 1, 2), ("attend", 3), ("forward", 1), ("attend", 4), ("relay", 1, -2),
    ("relay", 2, 1), ("relay", 0, 2), ("relay", 2, 2), ("relay", 0, -2), ("forward", 2),
    ("relay", 1, 3), ("relay", 2, -2), ("relay", 0, 3), ("forward", 3), ("relay", 4, 1),
    ("relay", 1, -3), ("launch", 3), ("forward", 4), ("relay", 4, -1), ("relay", 0, -3),
    ("relay", 2, -3), ("arrive", 1), ("relay", 2, 3), ("far", 1), ("relay", 3, -1),
    ("relay", 4, -2), ("relay", 4, 2), ("arrive", 0), ("far", 0), ("relay", 3, 1),
    ("arrive", 2), ("relay", 3, 2), ("far", 2), ("relay", 3, -2), ("relay", 4, -3),
    ("relay", 4, 3), ("far", 4), ("side", 5), ("relay", 3, 3), ("relay", 3, -3), ("near", 1),
    ("take", 1), ("relay", 5, 1), ("relay", 5, -1), ("relay", 5, -2), ("relay", 5, 2),
    ("arrive", 3), ("far", 3), ("near", 2), ("relay", 5, 3), ("relay", 5, -3), ("far", 5),
    ("take", 2), ("near", 4), ("take", 0), ("near", 0), ("near", 5), ("near", 3), ("take", 4),
    ("take", 3), ("take", 5),
)


def fused(
    depth,
    active_list,
    active_count,
    key_list,
    block_hbm,
    gate_ref,
    q_hbm,
    fresh_hbm,
    cache_hbm,
    w_hbm,
    out_ref,
    w_long,
    w_short,
    queries,
    fresh,
    cache,
    wide,
    keys,
    values,
    attended,
    mixed_in,
    pair_in,
    pair_out,
    sent,
    received,
    load_sem,
    own_sem,
    w_send,
    w_recv,
    kv_send,
    kv_recv,
    in_send,
    in_recv,
    a_send,
    a_recv,
    p_send,
    p_recv,
    out_send,
    out_recv,
):
    me = lax.axis_index("fsdp")
    z, x = me // LINE, me % LINE
    y = lax.axis_index("groups")
    b = lax.axis_index("blk")
    rows = w_hbm.shape[0]
    tok = q_hbm.shape[0]
    quarter = w_hbm.shape[1] // 4
    unit = quarter // UNITS
    tiles = active_list.shape[2]
    tile_rows = tok // tiles
    heads = q_hbm.shape[1] // HEAD_DIM
    sets = heads // GROUPED
    piece = PACK * HEAD_DIM
    pieces = heads // PACK
    listed = key_list.shape[0]

    def quarter_of(group, core):
        return pl.multiple_of((2 * group + core) * quarter, 128)

    mine = quarter_of(y, b)

    barrier = pltpu.get_barrier_semaphore()
    targets = (
        (z < depth - 1, {"fsdp": me + LINE}),
        (z > 0, {"fsdp": me - LINE}),
        (None, {"fsdp": z * LINE + 1 - x}),
    )
    twin = {"groups": 1 - y}
    core = {"blk": 1 - b}
    cross = {"groups": 1 - y, "blk": 1 - b}

    def when(cond, body):
        if cond is None:
            body()
        else:
            pl.when(cond)(body)

    def greet(device):
        pl.semaphore_signal(barrier, inc=1, device_id=device, device_id_type=MESH)

    for cond, device in targets + ((None, twin), (None, core), (None, cross)):
        when(cond, functools.partial(greet, device))

    def remote(src, dst, send, recv, device):
        return pltpu.make_async_remote_copy(
            src_ref=src,
            dst_ref=dst,
            send_sem=send,
            recv_sem=recv,
            device_id=device,
            device_id_type=MESH,
        )

    def extent(k):
        return (2 * k * unit, 2 * unit) if k < LONG else ((LONG + k) * unit, unit)

    def weight(k):
        return w_long.at[k] if k < LONG else w_short.at[k - LONG]

    def shard(k, s):
        return weight(k).at[pl.ds(pl.multiple_of(s * rows, 16), rows), :]

    def own_cols(k):
        low, size = extent(k)
        return w_hbm.at[:, pl.ds(pl.multiple_of(mine + low, 128), size)]

    streams = range(LONG + SHORT)

    loads = [
        pltpu.make_async_copy(fresh_hbm, fresh, load_sem.at[0]),
        pltpu.make_async_copy(cache_hbm, cache, load_sem.at[1]),
        pltpu.make_async_copy(q_hbm, queries, load_sem.at[2]),
        pltpu.make_async_copy(block_hbm, mixed_in, load_sem.at[3]),
    ]
    owns = [pltpu.make_async_copy(own_cols(k), shard(k, me), own_sem.at[k]) for k in streams]
    for load in loads[:3]:
        load.start()

    pl.semaphore_wait(barrier, 4 + (z > 0).astype(jnp.int32) + (z < depth - 1).astype(jnp.int32))

    swap_in = remote(
        block_hbm.at[:, pl.ds(quarter_of(y, 1 - b), quarter)],
        pair_in,
        in_send.at[0],
        in_recv.at[0],
        core,
    )

    def shard_copy(k, s, way, own=False):
        return remote(
            own_cols(k) if own else shard(k, s),
            shard(k, s),
            w_send.at[k, s, way],
            w_recv.at[k, s],
            targets[way][1],
        )

    def ways_of(k, dz, dx):
        if k < LONG and dx == 1:
            return []
        found = []
        if dz <= 0:
            found.append(0)
        if dz >= 0:
            found.append(1)
        if k < LONG or (dz, dx) == (0, 0):
            found.append(2)
        return found

    def inside(dz, body):
        if dz < 0:
            pl.when(z + dz >= 0)(body)
        elif dz > 0:
            pl.when(z + dz < depth)(body)
        else:
            body()

    def visit(k, dz, dx, done=False):
        s = (z + dz) * LINE + (x if dx == 0 else 1 - x)
        own = (dz, dx) == (0, 0)

        def body():
            if not done and not own:
                shard_copy(k, s, 2).wait_recv()

            def act(way):
                copy = shard_copy(k, s, way, own)
                if done:
                    copy.wait_send()
                else:
                    copy.start()

            for way in ways_of(k, dz, dx):
                when(targets[way][0], functools.partial(act, way))

        inside(dz, body)

    def launch(k):
        visit(k, 0, 0)

    def relay(k, dz):
        visit(k, dz, 0)
        if k >= LONG:
            visit(k, dz, 1)

    def side(k):
        visit(k, 0, 1)

    def arrive(k):
        visit(k, 0, 1)
        for far in range(1, depth):
            visit(k, -far, 1)
            visit(k, far, 1)

    def is_active(core_side, a):
        found = jnp.int32(0)
        for slot in range(tiles):
            hit = (active_list[0, core_side, slot] == a) & (slot < active_count[0, core_side])
            found = jnp.where(hit, jnp.int32(1), found)
        return found

    flags = [[is_active(core_side, a) for a in range(tiles)] for core_side in (b, 1 - b)]

    whole = pl.ds(pl.multiple_of(b * tok, 16), tok)

    def split_pair(g, i):
        for k in range(PACK):
            local_col = pl.multiple_of((i * PACK + k) * HEAD_DIM, 128)
            local_cols = pl.ds(local_col, HEAD_DIM)
            cols = pl.ds(pl.multiple_of(g * GROUPED * HEAD_DIM + local_col, 128), HEAD_DIM)
            for a in range(tiles):
                span = pl.ds(a * tile_rows, tile_rows)
                pair = jnp.where(flags[0][a] > 0, fresh[span, :, cols], cache[span, :, cols])
                pair = pair.reshape(2 * tile_rows, HEAD_DIM)
                wide[k, pl.ds(2 * a * tile_rows, 2 * tile_rows), :] = pair.astype(jnp.float32)
            keys[g][whole, local_cols] = wide[k, pl.ds(0, tok, 2), :].astype(jnp.bfloat16)
            values[g][whole, local_cols] = wide[k, pl.ds(1, tok, 2), :].astype(jnp.bfloat16)

    def kv_swap(g):
        return [
            remote(
                ref.at[whole, :], ref.at[whole, :], kv_send.at[j, g], kv_recv.at[j, g], core
            )
            for j, ref in enumerate((keys[g], values[g]))
        ]

    def is_listed(a, tile):
        found = jnp.int32(0)
        for t in range(listed):
            found = jnp.where(key_list[t, 0, b * tiles + a] == tile, jnp.int32(1), found)
        return found

    def tile_span(core_side, a):
        return pl.ds(pl.multiple_of(core_side * tok + a * tile_rows, 16), tile_rows)

    first_far, last_far = tile_span(1 - b, 0), tile_span(1 - b, 1)
    use_near = [is_listed(a, b * tiles + 1 - a) for a in range(tiles)]
    use_last = [is_listed(a, (1 - b) * tiles + 1) for a in range(tiles)]

    def three_tiles(ref, cols, a):
        spare = ref[first_far, cols]
        second = jnp.where(use_near[a] > 0, ref[tile_span(b, 1 - a), cols], spare)
        third = jnp.where(use_last[a] > 0, ref[last_far, cols], spare)
        return jnp.concatenate([ref[tile_span(b, a), cols], second, third], axis=0)

    factor = math.log2(math.e) / math.sqrt(HEAD_DIM)

    def rows_of(slot):
        return pl.ds(slot * tok, tok)

    def a_copies(n):
        cols = pl.ds(pl.multiple_of(n * piece, 128), piece)
        own = attended.at[rows_of(0), cols]
        over = attended.at[rows_of(2), cols]
        beside = attended.at[rows_of(1), cols]
        onward = attended.at[rows_of(3), cols]

        def lazy(j, src, dst, device):
            return lambda: remote(src, dst, a_send.at[j, n], a_recv.at[j, n], device)

        return lazy(0, own, over, twin), lazy(1, own, beside, core), lazy(2, over, onward, core)

    def attend(g, i):
        for k in range(PACK):
            local_col = pl.multiple_of((i * PACK + k) * HEAD_DIM, 128)
            local_cols = pl.ds(local_col, HEAD_DIM)
            cols = pl.ds(pl.multiple_of(g * GROUPED * HEAD_DIM + local_col, 128), HEAD_DIM)
            for a in range(tiles):
                query = queries[pl.ds(a * tile_rows, tile_rows), cols]
                key_rows = three_tiles(keys[g], local_cols, a)
                value_rows = three_tiles(values[g], local_cols, a)
                scores = lax.dot_general(
                    query, key_rows, (((1,), (1,)), ((), ())), preferred_element_type=jnp.float32
                )
                top = jnp.max(scores, axis=1, keepdims=True)
                terms = jnp.exp2((scores - top) * factor)
                total = jnp.sum(terms, axis=1, keepdims=True)
                summed = jnp.dot(
                    terms.astype(jnp.bfloat16), value_rows, preferred_element_type=jnp.float32
                )
                attended[pl.ds(a * tile_rows, tile_rows), cols] = (summed / total).astype(
                    jnp.bfloat16
                )
        n = g * (GROUPED // PACK) + i
        over, beside, _ = a_copies(n)
        over().start()
        beside().start()

    def attend_set(g):
        for copy in kv_swap(g):
            copy.wait_recv()
        pl.loop(0, GROUPED // PACK)(functools.partial(attend, g))

    def pass_on(low, high):
        @pl.loop(low, high)
        def _(n):
            over, _, onward = a_copies(n)
            over().wait_recv()
            onward().start()

    def p_copy(k, j):
        low, size = extent(k)
        part = (pl.ds(j * tok, tok), pl.ds(low, size))
        return remote(
            sent.at[part], received.at[part], p_send.at[k, j], p_recv.at[k, j], (twin, cross)[j]
        )

    def out_copy(k):
        low, size = extent(k)
        return remote(
            pair_out.at[:, pl.ds(low, size)],
            out_ref.at[:, pl.ds(pl.multiple_of(mine + low, 128), size)],
            out_send.at[k],
            out_recv.at[k],
            core,
        )

    def far_part(k):
        owns[k].wait()
        low, size = extent(k)
        for j in range(2):
            part = jnp.dot(
                attended[rows_of(2 + j), :], weight(k)[...], preferred_element_type=jnp.float32
            )
            sent[pl.ds(j * tok, tok), pl.ds(low, size)] = part.astype(jnp.bfloat16)
            p_copy(k, j).start()

    def blend(before, gate, part, flag):
        before = before.astype(jnp.float32)
        return jnp.where(flag > 0, before + gate * part, before).astype(jnp.bfloat16)

    def near_part(k):
        low, size = extent(k)
        cols = pl.ds(pl.multiple_of(mine + low, 128), size)
        gate = gate_ref[:, cols]
        part = jnp.dot(attended[rows_of(1), :], weight(k)[...], preferred_element_type=jnp.float32)
        for a in range(tiles):
            span = pl.ds(a * tile_rows, tile_rows)
            pair_out[span, pl.ds(low, size)] = blend(
                pair_in[span, pl.ds(low, size)],
                gate,
                part[a * tile_rows : (a + 1) * tile_rows],
                flags[1][a],
            )
        out_copy(k).start()
        part = jnp.dot(attended[rows_of(0), :], weight(k)[...], preferred_element_type=jnp.float32)
        for a in range(tiles):
            span = pl.ds(a * tile_rows, tile_rows)
            out_ref[span, cols] = blend(
                mixed_in[span, cols], gate, part[a * tile_rows : (a + 1) * tile_rows], flags[0][a]
            )

    def take(k):
        low, size = extent(k)
        for j in range(2):
            p_copy(k, j).wait_recv()
            base = quarter_of(1 - y, b if j == 0 else 1 - b)
            cols = pl.ds(pl.multiple_of(base + low, 128), size)
            gate = gate_ref[:, cols]
            for a in range(tiles):
                span = pl.ds(a * tile_rows, tile_rows)
                part = received[pl.ds(j * tok + a * tile_rows, tile_rows), pl.ds(low, size)]
                out_ref[span, cols] = blend(
                    mixed_in[span, cols], gate, part.astype(jnp.float32), flags[0][a]
                )

    def settle():
        for load in loads[:2]:
            load.wait()
        for g in range(sets):
            pl.loop(0, GROUPED // PACK)(functools.partial(split_pair, g))
            for copy in kv_swap(g):
                copy.start()
        loads[2].wait()
        for own in owns:
            own.start()
        loads[3].start()
        swap_in.start()

    def collect():
        @pl.loop(0, pieces)
        def _(n):
            _, beside, onward = a_copies(n)
            beside().wait_recv()
            onward().wait_recv()

        loads[3].wait()
        swap_in.wait_recv()

    share = pieces // sets
    steps = {
        "launch": launch,
        "settle": settle,
        "relay": relay,
        "side": side,
        "attend": attend_set,
        "forward": lambda g: pass_on(g * share, (g + 1) * share),
        "collect": collect,
        "arrive": arrive,
        "far": far_part,
        "near": near_part,
        "take": take,
    }
    late = False
    for name, *details in ORDER:
        if name in ("far", "near") and not late:
            collect()
            late = True
        steps[name](*details)

    swap_in.wait_send()
    for g in range(sets):
        for copy in kv_swap(g):
            copy.wait_send()

    @pl.loop(0, pieces)
    def _(n):
        for copy in a_copies(n):
            copy().wait_send()

    for k in streams:
        visit(k, 0, 0, done=True)
        if k >= LONG:
            visit(k, 0, 1, done=True)
        for far in range(1, depth):
            for dz in (-far, far):
                for dx in range(LINE if k >= LONG else 1):
                    visit(k, dz, dx, done=True)
        for j in range(2):
            p_copy(k, j).wait_send()
        out_copy(k).wait()


def local_fused(
    count,
    block_input,
    gate,
    q_fresh,
    kv_fresh,
    kv_cache,
    active_list,
    active_count,
    key_list,
    out_weight,
):
    tok, width = block_input.shape
    rows = out_weight.shape[0]
    quarter = width // 4
    unit = quarter // UNITS
    columns = q_fresh.shape[1]
    heads = columns // HEAD_DIM
    sets = heads // GROUPED
    pieces = heads // PACK
    streams = LONG + SHORT
    smem = pl.BlockSpec(memory_space=pltpu.SMEM)
    anywhere = pl.BlockSpec(memory_space=pltpu.HBM)
    dma = pltpu.SemaphoreType.DMA

    def vmem(*shape):
        return pltpu.VMEM(shape, jnp.bfloat16)

    return pl.pallas_call(
        functools.partial(fused, count // LINE),
        out_shape=pltpu.VMEM((tok, width), jnp.bfloat16),
        in_specs=[smem] * 3
        + [anywhere, pl.BlockSpec(memory_space=pltpu.VMEM)]
        + [anywhere] * 4,
        out_specs=pl.BlockSpec(memory_space=pltpu.VMEM),
        scratch_shapes=[
            vmem(LONG, count * rows, 2 * unit),
            vmem(SHORT, count * rows, unit),
            vmem(tok, columns),
            vmem(tok, 2, columns),
            vmem(tok, 2, columns),
            pltpu.VMEM((PACK, 2 * tok, HEAD_DIM), jnp.float32),
            [vmem(2 * tok, GROUPED * HEAD_DIM) for _ in range(sets)],
            [vmem(2 * tok, GROUPED * HEAD_DIM) for _ in range(sets)],
            vmem(4 * tok, columns),
            vmem(tok, width),
            vmem(tok, quarter),
            vmem(tok, quarter),
            vmem(2 * tok, quarter),
            vmem(2 * tok, quarter),
            dma((4,)),
            dma((streams,)),
            dma((streams, count, 3)),
            dma((streams, count)),
            dma((2, sets)),
            dma((2, sets)),
            dma((1,)),
            dma((1,)),
            dma((3, pieces)),
            dma((3, pieces)),
            dma((streams, 2)),
            dma((streams, 2)),
            dma((streams,)),
            dma((streams,)),
        ],
        compiler_params=pltpu.CompilerParams(
            collective_id=0, has_side_effects=True, vmem_limit_bytes=56000000
        ),
    )(
        active_list,
        active_count,
        key_list.transpose(2, 0, 1),
        block_input,
        gate[None, :],
        q_fresh,
        kv_fresh,
        kv_cache,
        out_weight,
    )


def per_device(groups, count, cores, *args):
    rows, width = args[-1].shape
    columns = args[2].shape[1]
    fits = groups == 2 and cores == 2 and count % LINE == 0 and rows % 16 == 0
    fits = fits and width % (4 * UNITS * 128) == 0 and count * rows * width < 1 << 24
    fits = fits and columns % (GROUPED * HEAD_DIM) == 0
    fits = fits and args[5].shape[2] == 2 and args[7].shape[1:] == (4, 3)
    return local_fused(count, *args) if fits else local(*args)


def solution(mesh):
    in_specs = (
        P(("groups", "fsdp", "blk"), None),
        P("groups"),
        P(("groups", "fsdp", "blk"), None),
        P(("groups", "fsdp", "blk"), None, None),
        P(("groups", "fsdp", "blk"), None, None),
        P(("groups", "fsdp"), None, None),
        P(("groups", "fsdp"), None),
        P(("groups", "fsdp"), None, None),
        P("fsdp", None),
    )
    sizes = [mesh.shape[axis] for axis in ("groups", "fsdp", "blk")]
    body = functools.partial(per_device, *sizes)
    out_specs = P(("groups", "fsdp", "blk"), None)
    return jax.shard_map(body, mesh=mesh, in_specs=in_specs, out_specs=out_specs, check_vma=False)
```

```python
import functools
import math

import jax
import jax.numpy as jnp
from jax import lax
from jax.experimental import pallas as pl
from jax.experimental.pallas import tpu as pltpu
from jax.sharding import PartitionSpec as P

HEADS = 20
HEAD_DIM = 128


MASKED = -1e30


def swapped(block, axis, apart):
    count = lax.axis_size(axis)
    route = []
    for low in range(count):
        high = low | 1 << apart
        if high != low and high < count:
            route += [(low, high), (high, low)]
    return lax.ppermute(block, axis, route)


def tile_flags(tile_list, tile_count):
    slot_ids = jnp.arange(tile_list.shape[0], dtype=jnp.int32)
    listed = (tile_list[:, None] == slot_ids[None, :]) & (slot_ids[:, None] < tile_count)
    return jnp.any(listed, axis=0)


def block_partial(query_tile, key_rows, value_rows, allowed):
    tile_rows = query_tile.shape[0]
    query3 = query_tile.reshape(tile_rows, HEADS, HEAD_DIM)
    key3 = key_rows.reshape(key_rows.shape[0], HEADS, HEAD_DIM)
    value3 = value_rows.reshape(value_rows.shape[0], HEADS, HEAD_DIM)
    scores = jnp.einsum(
        "qhd,khd->hqk", query3, key3, preferred_element_type=jnp.float32
    ) / math.sqrt(HEAD_DIM)
    scores = jnp.where(allowed[None, None, :], scores, MASKED)
    row_max = jnp.max(scores, axis=2)
    exp_terms = jnp.where(allowed[None, None, :], jnp.exp(scores - row_max[:, :, None]), 0.0)
    row_total = jnp.sum(exp_terms, axis=2)
    weights = exp_terms.astype(jnp.bfloat16)
    block_out = jnp.einsum("hqk,khd->hqd", weights, value3, preferred_element_type=jnp.float32)
    return (block_out, row_max, row_total)


def attend_block(
    queries, tile_list, tile_count, query_side, key_rows, value_rows, key_side, key_table
):
    tiles_dev = tile_list.shape[0]
    tile_rows = queries.shape[0] // tiles_dev
    slot_ids = jnp.arange(tiles_dev, dtype=jnp.int32)
    key_tiles = key_side * tiles_dev + slot_ids
    init_state = (
        jnp.zeros((tiles_dev, HEADS, tile_rows, HEAD_DIM), jnp.float32),
        jnp.full((tiles_dev, HEADS, tile_rows), MASKED, jnp.float32),
        jnp.zeros((tiles_dev, HEADS, tile_rows), jnp.float32),
    )

    def one_slot(slot_idx, carry_state):
        tile_pos = tile_list[slot_idx]
        query_tile = lax.dynamic_slice_in_dim(queries, tile_pos * tile_rows, tile_rows, 0)
        listed = key_table[query_side * tiles_dev + tile_pos]
        allowed_tiles = jnp.any(key_tiles[:, None] == listed[None, :], axis=1)
        allowed = jnp.repeat(allowed_tiles, tile_rows, total_repeat_length=tiles_dev * tile_rows)
        partial_value = block_partial(query_tile, key_rows, value_rows, allowed)
        return tuple(
            (whole.at[tile_pos].set(piece) for whole, piece in zip(carry_state, partial_value))
        )

    return lax.fori_loop(0, tile_count, one_slot, init_state)


def merge_states(earlier, later_state):
    out_one, max_one, total_one = earlier
    out_two, max_two, total_two = later_state
    joint_max = jnp.maximum(max_one, max_two)
    scale_one = jnp.exp(max_one - joint_max)
    scale_two = jnp.exp(max_two - joint_max)
    summed = out_one * scale_one[..., None] + out_two * scale_two[..., None]
    return (summed, total_one * scale_one + total_two * scale_two)


def local(
    block_input, gate, q_fresh, kv_fresh, kv_cache, active_list, active_count, key_list, out_weight
):
    own_side = lax.axis_index("blk")
    other_side = 1 - own_side
    tiles_dev = active_list.shape[2]
    tok_dev = block_input.shape[0]
    tile_rows = tok_dev // tiles_dev
    own_list = active_list[0, own_side]
    own_count = active_count[0, own_side]
    flags = tile_flags(own_list, own_count)
    row_flags = jnp.repeat(flags, tile_rows, total_repeat_length=tok_dev)
    resident = jnp.where(row_flags[:, None, None], kv_fresh, kv_cache)
    key_table = key_list[0]
    own_state = attend_block(
        q_fresh, own_list, own_count, own_side, resident[:, 0], resident[:, 1], own_side, key_table
    )
    other_kv = swapped(resident, "blk", 0)
    other_state = attend_block(
        q_fresh,
        own_list,
        own_count,
        own_side,
        other_kv[:, 0],
        other_kv[:, 1],
        other_side,
        key_table,
    )
    summed, denom = merge_states(own_state, other_state)
    denom = jnp.where(flags[:, None, None], denom, 1.0)
    attended = (
        (summed / denom[..., None])
        .transpose(0, 2, 1, 3)
        .reshape(tok_dev, HEADS * HEAD_DIM)
        .astype(jnp.bfloat16)
    )
    half_cols = out_weight.shape[1] // 2
    own_cols = lax.dynamic_slice_in_dim(out_weight, own_side * half_cols, half_cols, 1)
    half_weight = lax.all_gather(own_cols, "fsdp", axis=0, tiled=True)
    partner_rows = swapped(attended, "blk", 0)
    own_part = jnp.dot(attended, half_weight, preferred_element_type=jnp.float32)
    partner_part = jnp.dot(partner_rows, half_weight, preferred_element_type=jnp.float32)
    returned = swapped(partner_part, "blk", 0)
    projected = jnp.where(
        own_side == 0,
        jnp.concatenate([own_part, returned], axis=1),
        jnp.concatenate([returned, own_part], axis=1),
    )
    mixed = block_input.astype(jnp.float32) + gate[None, :] * projected
    return jnp.where(row_flags[:, None], mixed.astype(jnp.bfloat16), block_input)


MESH = pl.DeviceIdType.MESH
LINE = 2
DEPTH = 4
LONG, MIXED, SHORT = range(3)
STREAMS = ((LONG, 2), (LONG, 2), (LONG, 2), (LONG, 1), (LONG, 1), (SHORT, 1), (SHORT, 1))
UNITS = sum(size for _, size in STREAMS)
PACK = 2
GROUPED = 4
ORDER = (
    ("launch", 6), ("launch", 2), ("launch", 3), ("launch", 0), ("launch", 1), ("settle",),
    ("attend", 0), ("attend", 1), ("relay", 0, -1), ("side", 6), ("attend", 2),
    ("relay", 0, 1), ("relay", 2, 1), ("relay", 2, -1), ("attend", 3), ("relay", 0, 2),
    ("relay", 2, 2), ("relay", 0, 3), ("forward", 0), ("forward", 1), ("relay", 3, 1),
    ("forward", 2), ("relay", 3, -1), ("launch", 5), ("attend", 4), ("relay", 3, 2),
    ("relay", 1, -1), ("forward", 3), ("relay", 6, 1), ("relay", 2, 3), ("relay", 6, -1),
    ("relay", 3, 3), ("relay", 1, 1), ("forward", 4), ("far0", 0), ("relay", 6, 2),
    ("far1", 0), ("relay", 1, 2), ("launch", 4), ("far0", 2), ("begin", 6), ("near1", 0),
    ("far1", 2), ("far0", 3), ("side", 5), ("near0", 0), ("far1", 3), ("relay", 1, 3),
    ("take1", 0), ("near1", 2), ("relay", 4, -1), ("relay", 6, 3), ("take0", 0), ("near0", 2),
    ("near1", 3), ("far0", 6), ("relay", 4, 1), ("far1", 6), ("near1", 6), ("relay", 5, -1),
    ("relay", 4, 2), ("far0", 1), ("near0", 6), ("relay", 4, 3), ("relay", 5, 1), ("far1", 1),
    ("near0", 1), ("take0", 3), ("take1", 2), ("near0", 3), ("near1", 1), ("relay", 5, 2),
    ("far0", 4), ("far1", 4), ("near1", 4), ("begin", 5), ("take0", 2), ("drain_rest",),
    ("drain", 0), ("drain", 1), ("drain", 2), ("relay", 5, 3), ("far0", 5), ("take1", 1),
    ("take0", 1), ("far1", 5), ("take0", 4), ("near1", 5), ("near0", 5), ("take0", 6),
    ("take1", 6), ("near0", 4), ("take1", 4), ("take1", 3), ("take0", 5), ("take1", 5),
)


def fused(
    list_hbm,
    count_hbm,
    keys_hbm,
    block_hbm,
    gate_hbm,
    q_hbm,
    fresh_hbm,
    cache_hbm,
    w_hbm,
    out_ref,
    weights,
    queries,
    fresh,
    cache,
    wide,
    keys,
    values,
    attended,
    mixed_in,
    pair_in,
    pair_out,
    sent,
    received,
    sums,
    gate_ref,
    active_list,
    active_count,
    key_list,
    load_sem,
    own_sem,
    w_send,
    w_recv,
    kv_send,
    kv_recv,
    in_send,
    in_recv,
    a_send,
    a_recv,
    p_send,
    p_recv,
    out_send,
    out_recv,
):
    me = lax.axis_index("fsdp")
    z, x = me // LINE, me % LINE
    y = lax.axis_index("groups")
    b = lax.axis_index("blk")
    rows = w_hbm.shape[0]
    tok = q_hbm.shape[0]
    quarter = w_hbm.shape[1] // 4
    unit = quarter // UNITS
    tiles = active_list.shape[2]
    tile_rows = tok // tiles
    heads = q_hbm.shape[1] // HEAD_DIM
    sets = heads // GROUPED
    piece = PACK * HEAD_DIM
    pieces = heads // PACK
    listed = key_list.shape[0]

    def quarter_of(group, core):
        return pl.multiple_of((2 * group + core) * quarter, 128)

    mine = quarter_of(y, b)

    barrier = pltpu.get_barrier_semaphore()
    inward = jnp.where(z < DEPTH // 2, 1, -1)
    inner = (z > 0) & (z < DEPTH - 1)
    at_end = (z == 0) | (z == DEPTH - 1)
    targets = (
        (None, {"fsdp": me + inward * LINE}),
        (inner, {"fsdp": me - inward * LINE}),
        (None, {"fsdp": z * LINE + 1 - x}),
    )
    twin = {"groups": 1 - y}
    core = {"blk": 1 - b}
    cross = {"groups": 1 - y, "blk": 1 - b}

    def when(cond, body):
        if cond is None:
            body()
        else:
            pl.when(cond)(body)

    def greet(device):
        pl.semaphore_signal(barrier, inc=1, device_id=device, device_id_type=MESH)

    for cond, device in targets + ((None, twin), (None, core), (None, cross)):
        when(cond, functools.partial(greet, device))

    def remote(src, dst, send, recv, device):
        return pltpu.make_async_remote_copy(
            src_ref=src,
            dst_ref=dst,
            send_sem=send,
            recv_sem=recv,
            device_id=device,
            device_id_type=MESH,
        )

    def extent(k):
        return sum(size for _, size in STREAMS[:k]) * unit, STREAMS[k][1] * unit

    def shard(k, s):
        return weights[k].at[pl.ds(pl.multiple_of(s * rows, 16), rows), :]

    def own_cols(k):
        low, size = extent(k)
        return w_hbm.at[:, pl.ds(pl.multiple_of(mine + low, 128), size)]

    streams = range(len(STREAMS))

    loads = [
        pltpu.make_async_copy(fresh_hbm, fresh, load_sem.at[0]),
        pltpu.make_async_copy(cache_hbm, cache, load_sem.at[1]),
        pltpu.make_async_copy(q_hbm, queries, load_sem.at[2]),
        pltpu.make_async_copy(block_hbm, mixed_in, load_sem.at[3]),
        pltpu.make_async_copy(gate_hbm, gate_ref, load_sem.at[4]),
    ]
    small = [
        pltpu.make_async_copy(list_hbm, active_list, load_sem.at[5]),
        pltpu.make_async_copy(count_hbm, active_count, load_sem.at[6]),
        pltpu.make_async_copy(keys_hbm, key_list, load_sem.at[7]),
    ]
    owns = [pltpu.make_async_copy(own_cols(k), shard(k, me), own_sem.at[k]) for k in streams]
    for load in loads[:3] + small:
        load.start()

    pl.semaphore_wait(barrier, 5 + inner.astype(jnp.int32))

    swap_in = remote(
        block_hbm.at[:, pl.ds(quarter_of(y, 1 - b), quarter)],
        pair_in,
        in_send.at[0],
        in_recv.at[0],
        core,
    )

    def shard_copy(k, s, way, own=False):
        return remote(
            own_cols(k) if own else shard(k, s),
            shard(k, s),
            w_send.at[k, s, way],
            w_recv.at[k, s],
            targets[way][1],
        )

    def z_first(k, u):
        kind = STREAMS[k][0]
        return kind == LONG or (kind == MIXED and u == 3)

    places = {0: None, -1: inner, 1: None, 2: None, 3: at_end}

    def ways_of(k, u, dx):
        onward = dx == 0 or not (z_first(k, u) or (STREAMS[k][0] == MIXED and u == 2))
        found = []
        if onward and u in (0, -1):
            found.append(0)
        if onward and u in (0, 1, 2):
            found.append(1)
        if dx == 0 and (u == 0 or z_first(k, u)):
            found.append(2)
        return found

    def visit(k, u, dx, done=False):
        s = (z + inward * u) * LINE + (x if dx == 0 else 1 - x)
        own = (u, dx) == (0, 0)

        def body():
            if not done and not own:
                shard_copy(k, s, 2).wait_recv()

            def act(way):
                copy = shard_copy(k, s, way, own)
                if done:
                    copy.wait_send()
                else:
                    copy.start()

            for way in ways_of(k, u, dx):
                when(targets[way][0], functools.partial(act, way))

        when(places[u], body)

    def launch(k):
        visit(k, 0, 0)

    def relay(k, u, done=False):
        visit(k, u, 0, done)
        if not z_first(k, u):
            visit(k, u, 1, done)

    def side(k, done=False):
        visit(k, 0, 1, done)

    def arrive(k):
        def wait(u):
            s = (z + inward * u) * LINE + 1 - x
            shard_copy(k, s, 2).wait_recv()

        for u in (0, -1, 1, 2, 3):
            if z_first(k, u):
                when(places[u], functools.partial(wait, u))

    def is_active(core_side, a):
        found = jnp.int32(0)
        for slot in range(tiles):
            hit = (active_list[0, core_side, slot] == a) & (slot < active_count[0, core_side])
            found = jnp.where(hit, jnp.int32(1), found)
        return found

    flags = []

    whole = pl.ds(pl.multiple_of(b * tok, 16), tok)

    def split_pair(g, i):
        for k in range(PACK):
            local_col = pl.multiple_of((i * PACK + k) * HEAD_DIM, 128)
            local_cols = pl.ds(local_col, HEAD_DIM)
            cols = pl.ds(pl.multiple_of(g * GROUPED * HEAD_DIM + local_col, 128), HEAD_DIM)
            for a in range(tiles):
                span = pl.ds(a * tile_rows, tile_rows)
                pair = jnp.where(flags[0][a] > 0, fresh[span, :, cols], cache[span, :, cols])
                pair = pair.reshape(2 * tile_rows, HEAD_DIM)
                wide[k, pl.ds(2 * a * tile_rows, 2 * tile_rows), :] = pair.astype(jnp.float32)
            keys[g][whole, local_cols] = wide[k, pl.ds(0, tok, 2), :].astype(jnp.bfloat16)
            values[g][whole, local_cols] = wide[k, pl.ds(1, tok, 2), :].astype(jnp.bfloat16)

    def kv_swap(g):
        return [
            remote(
                ref.at[whole, :], ref.at[whole, :], kv_send.at[j, g], kv_recv.at[j, g], core
            )
            for j, ref in enumerate((keys[g], values[g]))
        ]

    def is_listed(a, tile):
        found = jnp.int32(0)
        for t in range(listed):
            found = jnp.where(key_list[t, 0, b * tiles + a] == tile, jnp.int32(1), found)
        return found

    def tile_span(core_side, a):
        return pl.ds(pl.multiple_of(core_side * tok + a * tile_rows, 16), tile_rows)

    first_far, last_far = tile_span(1 - b, 0), tile_span(1 - b, 1)
    use_near, use_last = [], []

    def three_tiles(ref, cols, a):
        spare = ref[first_far, cols]
        second = jnp.where(use_near[a] > 0, ref[tile_span(b, 1 - a), cols], spare)
        third = jnp.where(use_last[a] > 0, ref[last_far, cols], spare)
        return jnp.concatenate([ref[tile_span(b, a), cols], second, third], axis=0)

    factor = math.log2(math.e) / math.sqrt(HEAD_DIM)

    def rows_of(slot):
        return pl.ds(slot * tok, tok)

    def a_copies(n):
        cols = pl.ds(pl.multiple_of(n * piece, 128), piece)
        own = attended.at[rows_of(0), cols]
        over = attended.at[rows_of(2), cols]
        beside = attended.at[rows_of(1), cols]
        onward = attended.at[rows_of(3), cols]

        def lazy(j, src, dst, device):
            return lambda: remote(src, dst, a_send.at[j, n], a_recv.at[j, n], device)

        return lazy(0, own, over, twin), lazy(1, own, beside, core), lazy(2, over, onward, core)

    def attend(g, i):
        for k in range(PACK):
            local_col = pl.multiple_of((i * PACK + k) * HEAD_DIM, 128)
            local_cols = pl.ds(local_col, HEAD_DIM)
            cols = pl.ds(pl.multiple_of(g * GROUPED * HEAD_DIM + local_col, 128), HEAD_DIM)
            for a in range(tiles):
                query = queries[pl.ds(a * tile_rows, tile_rows), cols]
                key_rows = three_tiles(keys[g], local_cols, a)
                value_rows = three_tiles(values[g], local_cols, a)
                scores = lax.dot_general(
                    query, key_rows, (((1,), (1,)), ((), ())), preferred_element_type=jnp.float32
                )
                top = jnp.max(scores, axis=1, keepdims=True)
                terms = jnp.exp2((scores - top) * factor)
                total = jnp.sum(terms, axis=1, keepdims=True)
                summed = jnp.dot(
                    terms.astype(jnp.bfloat16), value_rows, preferred_element_type=jnp.float32
                )
                attended[pl.ds(a * tile_rows, tile_rows), cols] = (summed / total).astype(
                    jnp.bfloat16
                )
        n = g * (GROUPED // PACK) + i
        over, beside, _ = a_copies(n)
        over().start()
        beside().start()

    def attend_set(g):
        for copy in kv_swap(g):
            copy.wait_recv()
        pl.loop(0, GROUPED // PACK)(functools.partial(attend, g))

    def pass_on(low, high):
        @pl.loop(low, high)
        def _(n):
            over, _, onward = a_copies(n)
            over().wait_recv()
            onward().start()

    def p_copy(k, j):
        low, size = extent(k)
        part = (pl.ds(j * tok, tok), pl.ds(low, size))
        return remote(
            sent.at[part], received.at[part], p_send.at[k, j], p_recv.at[k, j], (cross, twin)[j]
        )

    def out_copy(k):
        low, size = extent(k)
        return remote(
            pair_out.at[:, pl.ds(low, size)],
            out_ref.at[:, pl.ds(pl.multiple_of(mine + low, 128), size)],
            out_send.at[k],
            out_recv.at[k],
            core,
        )

    span_rows = LINE * rows
    last_start = pl.multiple_of(jnp.where(z < DEPTH // 2, (DEPTH - 1) * span_rows, 0), 128)
    first_start = pl.multiple_of(jnp.where(z < DEPTH // 2, 0, span_rows), 128)
    begun = [details[0] for name, *details in ORDER if name == "begin"]
    early = dict(zip(begun, sums))

    def product(slot, k, start=None, depth=None):
        if depth is None:
            left, right = attended[rows_of(slot), :], weights[k][...]
        else:
            inner_span = pl.ds(start, depth)
            left, right = attended[rows_of(slot), inner_span], weights[k][inner_span, :]
        return jnp.dot(left, right, preferred_element_type=jnp.float32)

    def far_part(j, k):
        if j == 0:
            arrive(k)
            if k not in early:
                owns[k].wait()
        low, size = extent(k)
        if k in early:
            part = early[k][pl.ds(j * tok, tok), :] + product(3 - j, k, last_start, span_rows)
        else:
            part = product(3 - j, k)
        sent[pl.ds(j * tok, tok), pl.ds(low, size)] = part.astype(jnp.bfloat16)
        p_copy(k, j).start()

    def begin(k):
        owns[k].wait()
        for j in range(2):
            part = product(3 - j, k, first_start, (DEPTH - 1) * span_rows)
            early[k][pl.ds(j * tok, tok), :] = part

    def blend(before, gate, part, flag):
        before = before.astype(jnp.float32)
        return jnp.where(flag > 0, before + gate * part, before).astype(jnp.bfloat16)

    def near_part(j, k):
        low, size = extent(k)
        cols = pl.ds(pl.multiple_of(mine + low, 128), size)
        local_cols = pl.ds(low, size)
        gate = gate_ref[:, cols]
        part = product(1 - j, k)
        for a in range(tiles):
            span = pl.ds(a * tile_rows, tile_rows)
            term = part[a * tile_rows : (a + 1) * tile_rows]
            if j == 0:
                pair_out[span, local_cols] = blend(
                    pair_in[span, local_cols], gate, term, flags[1][a]
                )
            else:
                out_ref[span, cols] = blend(mixed_in[span, cols], gate, term, flags[0][a])
        if j == 0:
            out_copy(k).start()

    def take(j, k):
        low, size = extent(k)
        p_copy(k, j).wait_recv()
        base = quarter_of(1 - y, b if j == 1 else 1 - b)
        cols = pl.ds(pl.multiple_of(base + low, 128), size)
        gate = gate_ref[:, cols]
        for a in range(tiles):
            span = pl.ds(a * tile_rows, tile_rows)
            part = received[pl.ds(j * tok + a * tile_rows, tile_rows), pl.ds(low, size)]
            out_ref[span, cols] = blend(
                mixed_in[span, cols], gate, part.astype(jnp.float32), flags[0][a]
            )

    def settle():
        for load in small:
            load.wait()
        for core_side in (b, 1 - b):
            flags.append([is_active(core_side, a) for a in range(tiles)])
        for a in range(tiles):
            use_near.append(is_listed(a, b * tiles + 1 - a))
            use_last.append(is_listed(a, (1 - b) * tiles + 1))
        for load in loads[:2]:
            load.wait()
        for g in range(sets):
            pl.loop(0, GROUPED // PACK)(functools.partial(split_pair, g))
            for copy in kv_swap(g):
                copy.start()
        loads[2].wait()
        for own in owns:
            own.start()
        for load in loads[3:]:
            load.start()
        swap_in.start()

    def collect():
        @pl.loop(0, pieces)
        def _(n):
            _, beside, onward = a_copies(n)
            beside().wait_recv()
            onward().wait_recv()

        for load in loads[3:]:
            load.wait()
        swap_in.wait_recv()

    def drain_rest():
        swap_in.wait_send()
        for g in range(sets):
            for copy in kv_swap(g):
                copy.wait_send()

        @pl.loop(0, pieces)
        def _(n):
            for copy in a_copies(n):
                copy().wait_send()

    def drain(k):
        visit(k, 0, 0, done=True)
        if not z_first(k, 0):
            side(k, done=True)
        for u in (-1, 1, 2, 3):
            relay(k, u, done=True)

    share = pieces // sets
    steps = {
        "launch": launch,
        "settle": settle,
        "relay": relay,
        "side": side,
        "attend": attend_set,
        "forward": lambda g: pass_on(g * share, (g + 1) * share),
        "begin": begin,
        "far0": functools.partial(far_part, 0),
        "far1": functools.partial(far_part, 1),
        "near0": functools.partial(near_part, 0),
        "near1": functools.partial(near_part, 1),
        "take0": functools.partial(take, 0),
        "take1": functools.partial(take, 1),
        "drain": drain,
        "drain_rest": drain_rest,
    }
    collected = False
    for name, *details in ORDER:
        if name in ("begin", "far0") and not collected:
            collect()
            collected = True
        steps[name](*details)

    drained = [details[0] for name, *details in ORDER if name == "drain"]
    if ("drain_rest",) not in ORDER:
        drain_rest()
    for k in streams:
        if k not in drained:
            drain(k)
        for j in range(2):
            p_copy(k, j).wait_send()
        out_copy(k).wait()


def local_fused(
    count,
    block_input,
    gate,
    q_fresh,
    kv_fresh,
    kv_cache,
    active_list,
    active_count,
    key_list,
    out_weight,
):
    tok, width = block_input.shape
    rows = out_weight.shape[0]
    quarter = width // 4
    unit = quarter // UNITS
    columns = q_fresh.shape[1]
    heads = columns // HEAD_DIM
    sets = heads // GROUPED
    pieces = heads // PACK
    streams = len(STREAMS)
    anywhere = pl.BlockSpec(memory_space=pltpu.HBM)
    dma = pltpu.SemaphoreType.DMA

    def vmem(*shape):
        return pltpu.VMEM(shape, jnp.bfloat16)

    return pl.pallas_call(
        fused,
        out_shape=pltpu.VMEM((tok, width), jnp.bfloat16),
        in_specs=[anywhere] * 9,
        out_specs=pl.BlockSpec(memory_space=pltpu.VMEM),
        scratch_shapes=[
            [vmem(count * rows, size * unit) for _, size in STREAMS],
            vmem(tok, columns),
            vmem(tok, 2, columns),
            vmem(tok, 2, columns),
            pltpu.VMEM((PACK, 2 * tok, HEAD_DIM), jnp.float32),
            [vmem(2 * tok, GROUPED * HEAD_DIM) for _ in range(sets)],
            [vmem(2 * tok, GROUPED * HEAD_DIM) for _ in range(sets)],
            vmem(4 * tok, columns),
            vmem(tok, width),
            vmem(tok, quarter),
            vmem(tok, quarter),
            vmem(2 * tok, quarter),
            vmem(2 * tok, quarter),
            [
                pltpu.VMEM((2 * tok, STREAMS[details[0]][1] * unit), jnp.float32)
                for name, *details in ORDER
                if name == "begin"
            ],
            pltpu.VMEM((1, width), jnp.float32),
            pltpu.SMEM(active_list.shape, jnp.int32),
            pltpu.SMEM(active_count.shape, jnp.int32),
            pltpu.SMEM((key_list.shape[2],) + key_list.shape[:2], jnp.int32),
            dma((8,)),
            dma((streams,)),
            dma((streams, count, 3)),
            dma((streams, count)),
            dma((2, sets)),
            dma((2, sets)),
            dma((1,)),
            dma((1,)),
            dma((3, pieces)),
            dma((3, pieces)),
            dma((streams, 2)),
            dma((streams, 2)),
            dma((streams,)),
            dma((streams,)),
        ],
        compiler_params=pltpu.CompilerParams(
            collective_id=0, has_side_effects=True, vmem_limit_bytes=56000000
        ),
    )(
        active_list,
        active_count,
        key_list.transpose(2, 0, 1),
        block_input,
        gate[None, :],
        q_fresh,
        kv_fresh,
        kv_cache,
        out_weight,
    )


def per_device(groups, count, cores, *args):
    rows, width = args[-1].shape
    columns = args[2].shape[1]
    fits = groups == 2 and cores == 2 and count == DEPTH * LINE and rows % 16 == 0
    fits = fits and width % (4 * UNITS * 128) == 0 and count * rows * width < 1 << 24
    fits = fits and columns % (GROUPED * HEAD_DIM) == 0 and LINE * rows % 128 == 0
    fits = fits and args[5].shape[2] == 2 and args[7].shape[1:] == (4, 3)
    return local_fused(count, *args) if fits else local(*args)


def solution(mesh):
    in_specs = (
        P(("groups", "fsdp", "blk"), None),
        P("groups"),
        P(("groups", "fsdp", "blk"), None),
        P(("groups", "fsdp", "blk"), None, None),
        P(("groups", "fsdp", "blk"), None, None),
        P(("groups", "fsdp"), None, None),
        P(("groups", "fsdp"), None),
        P(("groups", "fsdp"), None, None),
        P("fsdp", None),
    )
    sizes = [mesh.shape[axis] for axis in ("groups", "fsdp", "blk")]
    body = functools.partial(per_device, *sizes)
    out_specs = P(("groups", "fsdp", "blk"), None)
    return jax.shard_map(body, mesh=mesh, in_specs=in_specs, out_specs=out_specs, check_vma=False)
```

```python
import functools
import math

import jax
import jax.numpy as jnp
from jax import lax
from jax.experimental import pallas as pl
from jax.experimental.pallas import tpu as pltpu
from jax.sharding import PartitionSpec as P

HEADS = 20
HEAD_DIM = 128


MASKED = -1e30


def swapped(block, axis, apart):
    count = lax.axis_size(axis)
    route = []
    for low in range(count):
        high = low | 1 << apart
        if high != low and high < count:
            route += [(low, high), (high, low)]
    return lax.ppermute(block, axis, route)


def tile_flags(tile_list, tile_count):
    slot_ids = jnp.arange(tile_list.shape[0], dtype=jnp.int32)
    listed = (tile_list[:, None] == slot_ids[None, :]) & (slot_ids[:, None] < tile_count)
    return jnp.any(listed, axis=0)


def block_partial(query_tile, key_rows, value_rows, allowed):
    tile_rows = query_tile.shape[0]
    query3 = query_tile.reshape(tile_rows, HEADS, HEAD_DIM)
    key3 = key_rows.reshape(key_rows.shape[0], HEADS, HEAD_DIM)
    value3 = value_rows.reshape(value_rows.shape[0], HEADS, HEAD_DIM)
    scores = jnp.einsum(
        "qhd,khd->hqk", query3, key3, preferred_element_type=jnp.float32
    ) / math.sqrt(HEAD_DIM)
    scores = jnp.where(allowed[None, None, :], scores, MASKED)
    row_max = jnp.max(scores, axis=2)
    exp_terms = jnp.where(allowed[None, None, :], jnp.exp(scores - row_max[:, :, None]), 0.0)
    row_total = jnp.sum(exp_terms, axis=2)
    weights = exp_terms.astype(jnp.bfloat16)
    block_out = jnp.einsum("hqk,khd->hqd", weights, value3, preferred_element_type=jnp.float32)
    return (block_out, row_max, row_total)


def attend_block(
    queries, tile_list, tile_count, query_side, key_rows, value_rows, key_side, key_table
):
    tiles_dev = tile_list.shape[0]
    tile_rows = queries.shape[0] // tiles_dev
    slot_ids = jnp.arange(tiles_dev, dtype=jnp.int32)
    key_tiles = key_side * tiles_dev + slot_ids
    init_state = (
        jnp.zeros((tiles_dev, HEADS, tile_rows, HEAD_DIM), jnp.float32),
        jnp.full((tiles_dev, HEADS, tile_rows), MASKED, jnp.float32),
        jnp.zeros((tiles_dev, HEADS, tile_rows), jnp.float32),
    )

    def one_slot(slot_idx, carry_state):
        tile_pos = tile_list[slot_idx]
        query_tile = lax.dynamic_slice_in_dim(queries, tile_pos * tile_rows, tile_rows, 0)
        listed = key_table[query_side * tiles_dev + tile_pos]
        allowed_tiles = jnp.any(key_tiles[:, None] == listed[None, :], axis=1)
        allowed = jnp.repeat(allowed_tiles, tile_rows, total_repeat_length=tiles_dev * tile_rows)
        partial_value = block_partial(query_tile, key_rows, value_rows, allowed)
        return tuple(
            (whole.at[tile_pos].set(piece) for whole, piece in zip(carry_state, partial_value))
        )

    return lax.fori_loop(0, tile_count, one_slot, init_state)


def merge_states(earlier, later_state):
    out_one, max_one, total_one = earlier
    out_two, max_two, total_two = later_state
    joint_max = jnp.maximum(max_one, max_two)
    scale_one = jnp.exp(max_one - joint_max)
    scale_two = jnp.exp(max_two - joint_max)
    summed = out_one * scale_one[..., None] + out_two * scale_two[..., None]
    return (summed, total_one * scale_one + total_two * scale_two)


def local(
    block_input, gate, q_fresh, kv_fresh, kv_cache, active_list, active_count, key_list, out_weight
):
    own_side = lax.axis_index("blk")
    other_side = 1 - own_side
    tiles_dev = active_list.shape[2]
    tok_dev = block_input.shape[0]
    tile_rows = tok_dev // tiles_dev
    own_list = active_list[0, own_side]
    own_count = active_count[0, own_side]
    flags = tile_flags(own_list, own_count)
    row_flags = jnp.repeat(flags, tile_rows, total_repeat_length=tok_dev)
    resident = jnp.where(row_flags[:, None, None], kv_fresh, kv_cache)
    key_table = key_list[0]
    own_state = attend_block(
        q_fresh, own_list, own_count, own_side, resident[:, 0], resident[:, 1], own_side, key_table
    )
    other_kv = swapped(resident, "blk", 0)
    other_state = attend_block(
        q_fresh,
        own_list,
        own_count,
        own_side,
        other_kv[:, 0],
        other_kv[:, 1],
        other_side,
        key_table,
    )
    summed, denom = merge_states(own_state, other_state)
    denom = jnp.where(flags[:, None, None], denom, 1.0)
    attended = (
        (summed / denom[..., None])
        .transpose(0, 2, 1, 3)
        .reshape(tok_dev, HEADS * HEAD_DIM)
        .astype(jnp.bfloat16)
    )
    half_cols = out_weight.shape[1] // 2
    own_cols = lax.dynamic_slice_in_dim(out_weight, own_side * half_cols, half_cols, 1)
    half_weight = lax.all_gather(own_cols, "fsdp", axis=0, tiled=True)
    partner_rows = swapped(attended, "blk", 0)
    own_part = jnp.dot(attended, half_weight, preferred_element_type=jnp.float32)
    partner_part = jnp.dot(partner_rows, half_weight, preferred_element_type=jnp.float32)
    returned = swapped(partner_part, "blk", 0)
    projected = jnp.where(
        own_side == 0,
        jnp.concatenate([own_part, returned], axis=1),
        jnp.concatenate([returned, own_part], axis=1),
    )
    mixed = block_input.astype(jnp.float32) + gate[None, :] * projected
    return jnp.where(row_flags[:, None], mixed.astype(jnp.bfloat16), block_input)


MESH = pl.DeviceIdType.MESH
LINE = 2
DEPTH = 4
LONG, MIXED, SHORT = range(3)
STREAMS = ((LONG, 2), (LONG, 2), (LONG, 2), (LONG, 1), (LONG, 1), (SHORT, 1), (SHORT, 1))
UNITS = sum(size for _, size in STREAMS)
PACK = 2
GROUPED = 4
ORDER = (
    ("launch", 4), ("launch", 6), ("launch", 0), ("settle",), ("relay", 4, -1), ("launch", 2),
    ("launch", 1), ("relay", 4, 1), ("attend", 0), ("relay", 0, 1), ("side", 6), ("attend", 1),
    ("attend", 2), ("relay", 0, -1), ("attend", 3), ("forward", 0), ("relay", 2, 1),
    ("relay", 2, -1), ("relay", 0, 2), ("relay", 4, 2), ("forward", 1), ("launch", 5),
    ("forward", 2), ("relay", 2, 2), ("relay", 6, -1), ("relay", 6, 1), ("attend", 4),
    ("forward", 3), ("relay", 1, -1), ("relay", 0, 3), ("relay", 4, 3), ("relay", 2, 3),
    ("relay", 1, 1), ("forward", 4), ("far0", 0), ("far1", 0), ("near1", 0), ("relay", 1, 2),
    ("launch", 3), ("far0", 2), ("near1", 2), ("relay", 6, 2), ("begin", 6), ("far1", 2),
    ("side", 5), ("far0", 4), ("relay", 1, 3), ("far1", 4), ("relay", 6, 3), ("relay", 3, 1),
    ("far0", 6), ("relay", 3, -1), ("near0", 6), ("near1", 4), ("near0", 2), ("far1", 6),
    ("near0", 0), ("relay", 3, 2), ("relay", 5, 1), ("relay", 5, -1), ("far0", 1),
    ("take0", 4), ("take0", 0), ("take1", 4), ("relay", 3, 3), ("take0", 2), ("near0", 1),
    ("far1", 1), ("near1", 1), ("take0", 6), ("near1", 6), ("relay", 5, 2), ("take1", 0),
    ("far0", 3), ("far1", 3), ("take1", 2), ("begin", 5), ("near0", 4), ("drain_rest",),
    ("drain", 0), ("drain", 1), ("drain", 2), ("relay", 5, 3), ("far0", 5), ("near0", 5),
    ("near1", 3), ("far1", 5), ("take0", 1), ("take1", 1), ("near0", 3), ("take1", 6),
    ("take0", 3), ("take1", 3), ("near1", 5), ("drain", 3), ("drain", 4), ("drain", 5),
    ("drain", 6), ("take0", 5), ("take1", 5),
)


def fused(
    list_hbm,
    count_hbm,
    keys_hbm,
    block_hbm,
    gate_hbm,
    q_hbm,
    fresh_hbm,
    cache_hbm,
    w_hbm,
    out_ref,
    weights,
    queries,
    fresh,
    cache,
    wide,
    keys,
    values,
    attended,
    mixed_in,
    pair_in,
    pair_out,
    sent,
    received,
    sums,
    gate_ref,
    active_list,
    active_count,
    key_list,
    load_sem,
    own_sem,
    w_send,
    w_recv,
    kv_send,
    kv_recv,
    in_send,
    in_recv,
    a_send,
    a_recv,
    p_send,
    p_recv,
    out_send,
    out_recv,
):
    me = lax.axis_index("fsdp")
    z, x = me // LINE, me % LINE
    y = lax.axis_index("groups")
    b = lax.axis_index("blk")
    rows = w_hbm.shape[0]
    tok = q_hbm.shape[0]
    quarter = w_hbm.shape[1] // 4
    unit = quarter // UNITS
    tiles = active_list.shape[2]
    tile_rows = tok // tiles
    heads = q_hbm.shape[1] // HEAD_DIM
    sets = heads // GROUPED
    piece = PACK * HEAD_DIM
    pieces = heads // PACK
    listed = key_list.shape[0]

    def quarter_of(group, core):
        return pl.multiple_of((2 * group + core) * quarter, 128)

    mine = quarter_of(y, b)

    barrier = pltpu.get_barrier_semaphore()
    inward = jnp.where(z < DEPTH // 2, 1, -1)
    inner = (z > 0) & (z < DEPTH - 1)
    at_end = (z == 0) | (z == DEPTH - 1)
    targets = (
        (None, {"fsdp": me + inward * LINE}),
        (inner, {"fsdp": me - inward * LINE}),
        (None, {"fsdp": z * LINE + 1 - x}),
    )
    twin = {"groups": 1 - y}
    core = {"blk": 1 - b}
    cross = {"groups": 1 - y, "blk": 1 - b}

    def when(cond, body):
        if cond is None:
            body()
        else:
            pl.when(cond)(body)

    def greet(device):
        pl.semaphore_signal(barrier, inc=1, device_id=device, device_id_type=MESH)

    for cond, device in targets + ((None, twin), (None, core), (None, cross)):
        when(cond, functools.partial(greet, device))

    def remote(src, dst, send, recv, device):
        return pltpu.make_async_remote_copy(
            src_ref=src,
            dst_ref=dst,
            send_sem=send,
            recv_sem=recv,
            device_id=device,
            device_id_type=MESH,
        )

    def extent(k):
        return sum(size for _, size in STREAMS[:k]) * unit, STREAMS[k][1] * unit

    def shard(k, s):
        return weights[k].at[pl.ds(pl.multiple_of(s * rows, 16), rows), :]

    def own_cols(k):
        low, size = extent(k)
        return w_hbm.at[:, pl.ds(pl.multiple_of(mine + low, 128), size)]

    streams = range(len(STREAMS))

    loads = [
        pltpu.make_async_copy(fresh_hbm, fresh, load_sem.at[0]),
        pltpu.make_async_copy(cache_hbm, cache, load_sem.at[1]),
        pltpu.make_async_copy(q_hbm, queries, load_sem.at[2]),
        pltpu.make_async_copy(block_hbm, mixed_in, load_sem.at[3]),
        pltpu.make_async_copy(gate_hbm, gate_ref, load_sem.at[4]),
    ]
    small = [
        pltpu.make_async_copy(list_hbm, active_list, load_sem.at[5]),
        pltpu.make_async_copy(count_hbm, active_count, load_sem.at[6]),
        pltpu.make_async_copy(keys_hbm, key_list, load_sem.at[7]),
    ]
    owns = [pltpu.make_async_copy(own_cols(k), shard(k, me), own_sem.at[k]) for k in streams]
    for load in loads[:3] + small:
        load.start()

    pl.semaphore_wait(barrier, 5 + inner.astype(jnp.int32))

    swap_in = remote(
        block_hbm.at[:, pl.ds(quarter_of(y, 1 - b), quarter)],
        pair_in,
        in_send.at[0],
        in_recv.at[0],
        core,
    )

    def shard_copy(k, s, way, own=False):
        return remote(
            own_cols(k) if own else shard(k, s),
            shard(k, s),
            w_send.at[k, s, way],
            w_recv.at[k, s],
            targets[way][1],
        )

    def z_first(k, u):
        kind = STREAMS[k][0]
        return kind == LONG or (kind == MIXED and u == 3)

    places = {0: None, -1: inner, 1: None, 2: None, 3: at_end}

    def ways_of(k, u, dx):
        onward = dx == 0 or not (z_first(k, u) or (STREAMS[k][0] == MIXED and u == 2))
        found = []
        if onward and u in (0, -1):
            found.append(0)
        if onward and u in (0, 1, 2):
            found.append(1)
        if dx == 0 and (u == 0 or z_first(k, u)):
            found.append(2)
        return found

    def visit(k, u, dx, done=False):
        s = (z + inward * u) * LINE + (x if dx == 0 else 1 - x)
        own = (u, dx) == (0, 0)

        def body():
            if not done and not own:
                shard_copy(k, s, 2).wait_recv()

            def act(way):
                copy = shard_copy(k, s, way, own)
                if done:
                    copy.wait_send()
                else:
                    copy.start()

            for way in ways_of(k, u, dx):
                when(targets[way][0], functools.partial(act, way))

        when(places[u], body)

    def launch(k):
        visit(k, 0, 0)

    def relay(k, u, done=False):
        visit(k, u, 0, done)
        if not z_first(k, u):
            visit(k, u, 1, done)

    def side(k, done=False):
        visit(k, 0, 1, done)

    def arrive(k):
        def wait(u):
            s = (z + inward * u) * LINE + 1 - x
            shard_copy(k, s, 2).wait_recv()

        for u in (0, -1, 1, 2, 3):
            if z_first(k, u):
                when(places[u], functools.partial(wait, u))

    def is_active(core_side, a):
        found = jnp.int32(0)
        for slot in range(tiles):
            hit = (active_list[0, core_side, slot] == a) & (slot < active_count[0, core_side])
            found = jnp.where(hit, jnp.int32(1), found)
        return found

    flags = []

    whole = pl.ds(pl.multiple_of(b * tok, 16), tok)

    def split_pair(g, i):
        for k in range(PACK):
            local_col = pl.multiple_of((i * PACK + k) * HEAD_DIM, 128)
            local_cols = pl.ds(local_col, HEAD_DIM)
            cols = pl.ds(pl.multiple_of(g * GROUPED * HEAD_DIM + local_col, 128), HEAD_DIM)
            for a in range(tiles):
                span = pl.ds(a * tile_rows, tile_rows)
                pair = jnp.where(flags[0][a] > 0, fresh[span, :, cols], cache[span, :, cols])
                pair = pair.reshape(2 * tile_rows, HEAD_DIM)
                wide[k, pl.ds(2 * a * tile_rows, 2 * tile_rows), :] = pair.astype(jnp.float32)
            keys[g][whole, local_cols] = wide[k, pl.ds(0, tok, 2), :].astype(jnp.bfloat16)
            values[g][whole, local_cols] = wide[k, pl.ds(1, tok, 2), :].astype(jnp.bfloat16)

    def kv_swap(g):
        return [
            remote(
                ref.at[whole, :], ref.at[whole, :], kv_send.at[j, g], kv_recv.at[j, g], core
            )
            for j, ref in enumerate((keys[g], values[g]))
        ]

    def is_listed(a, tile):
        found = jnp.int32(0)
        for t in range(listed):
            found = jnp.where(key_list[t, 0, b * tiles + a] == tile, jnp.int32(1), found)
        return found

    def tile_span(core_side, a):
        return pl.ds(pl.multiple_of(core_side * tok + a * tile_rows, 16), tile_rows)

    first_far, last_far = tile_span(1 - b, 0), tile_span(1 - b, 1)
    use_near, use_last = [], []

    def three_tiles(ref, cols, a):
        spare = ref[first_far, cols]
        second = jnp.where(use_near[a] > 0, ref[tile_span(b, 1 - a), cols], spare)
        third = jnp.where(use_last[a] > 0, ref[last_far, cols], spare)
        return jnp.concatenate([ref[tile_span(b, a), cols], second, third], axis=0)

    factor = math.log2(math.e) / math.sqrt(HEAD_DIM)

    def rows_of(slot):
        return pl.ds(slot * tok, tok)

    def a_copies(n):
        cols = pl.ds(pl.multiple_of(n * piece, 128), piece)
        own = attended.at[rows_of(0), cols]
        over = attended.at[rows_of(2), cols]
        beside = attended.at[rows_of(1), cols]
        onward = attended.at[rows_of(3), cols]

        def lazy(j, src, dst, device):
            return lambda: remote(src, dst, a_send.at[j, n], a_recv.at[j, n], device)

        return lazy(0, own, over, twin), lazy(1, own, beside, core), lazy(2, over, onward, core)

    def attend(g, i):
        for k in range(PACK):
            local_col = pl.multiple_of((i * PACK + k) * HEAD_DIM, 128)
            local_cols = pl.ds(local_col, HEAD_DIM)
            cols = pl.ds(pl.multiple_of(g * GROUPED * HEAD_DIM + local_col, 128), HEAD_DIM)
            for a in range(tiles):
                query = queries[pl.ds(a * tile_rows, tile_rows), cols]
                key_rows = three_tiles(keys[g], local_cols, a)
                value_rows = three_tiles(values[g], local_cols, a)
                scores = lax.dot_general(
                    query, key_rows, (((1,), (1,)), ((), ())), preferred_element_type=jnp.float32
                )
                top = jnp.max(scores, axis=1, keepdims=True)
                terms = jnp.exp2((scores - top) * factor)
                total = jnp.sum(terms, axis=1, keepdims=True)
                summed = jnp.dot(
                    terms.astype(jnp.bfloat16), value_rows, preferred_element_type=jnp.float32
                )
                attended[pl.ds(a * tile_rows, tile_rows), cols] = (summed / total).astype(
                    jnp.bfloat16
                )
        n = g * (GROUPED // PACK) + i
        over, beside, _ = a_copies(n)
        over().start()
        beside().start()

    def attend_set(g):
        for copy in kv_swap(g):
            copy.wait_recv()
        pl.loop(0, GROUPED // PACK)(functools.partial(attend, g))

    def pass_on(low, high):
        @pl.loop(low, high)
        def _(n):
            over, _, onward = a_copies(n)
            over().wait_recv()
            onward().start()

    def p_copy(k, j):
        low, size = extent(k)
        part = (pl.ds(j * tok, tok), pl.ds(low, size))
        return remote(
            sent.at[part], received.at[part], p_send.at[k, j], p_recv.at[k, j], (cross, twin)[j]
        )

    def out_copy(k):
        low, size = extent(k)
        return remote(
            pair_out.at[:, pl.ds(low, size)],
            out_ref.at[:, pl.ds(pl.multiple_of(mine + low, 128), size)],
            out_send.at[k],
            out_recv.at[k],
            core,
        )

    span_rows = LINE * rows
    last_start = pl.multiple_of(jnp.where(z < DEPTH // 2, (DEPTH - 1) * span_rows, 0), 128)
    first_start = pl.multiple_of(jnp.where(z < DEPTH // 2, 0, span_rows), 128)
    begun = [details[0] for name, *details in ORDER if name == "begin"]
    early = dict(zip(begun, sums))

    def product(slot, k, start=None, depth=None):
        if depth is None:
            left, right = attended[rows_of(slot), :], weights[k][...]
        else:
            inner_span = pl.ds(start, depth)
            left, right = attended[rows_of(slot), inner_span], weights[k][inner_span, :]
        return jnp.dot(left, right, preferred_element_type=jnp.float32)

    def far_part(j, k):
        if j == 0:
            arrive(k)
            if k not in early:
                owns[k].wait()
        low, size = extent(k)
        if k in early:
            part = early[k][pl.ds(j * tok, tok), :] + product(3 - j, k, last_start, span_rows)
        else:
            part = product(3 - j, k)
        sent[pl.ds(j * tok, tok), pl.ds(low, size)] = part.astype(jnp.bfloat16)
        p_copy(k, j).start()

    def begin(k):
        owns[k].wait()
        for j in range(2):
            part = product(3 - j, k, first_start, (DEPTH - 1) * span_rows)
            early[k][pl.ds(j * tok, tok), :] = part

    def blend(before, gate, part, flag):
        before = before.astype(jnp.float32)
        return jnp.where(flag > 0, before + gate * part, before).astype(jnp.bfloat16)

    def near_part(j, k):
        low, size = extent(k)
        cols = pl.ds(pl.multiple_of(mine + low, 128), size)
        local_cols = pl.ds(low, size)
        gate = gate_ref[:, cols]
        part = product(1 - j, k)
        for a in range(tiles):
            span = pl.ds(a * tile_rows, tile_rows)
            term = part[a * tile_rows : (a + 1) * tile_rows]
            if j == 0:
                pair_out[span, local_cols] = blend(
                    pair_in[span, local_cols], gate, term, flags[1][a]
                )
            else:
                out_ref[span, cols] = blend(mixed_in[span, cols], gate, term, flags[0][a])
        if j == 0:
            out_copy(k).start()

    def take(j, k):
        low, size = extent(k)
        p_copy(k, j).wait_recv()
        base = quarter_of(1 - y, b if j == 1 else 1 - b)
        cols = pl.ds(pl.multiple_of(base + low, 128), size)
        gate = gate_ref[:, cols]
        for a in range(tiles):
            span = pl.ds(a * tile_rows, tile_rows)
            part = received[pl.ds(j * tok + a * tile_rows, tile_rows), pl.ds(low, size)]
            out_ref[span, cols] = blend(
                mixed_in[span, cols], gate, part.astype(jnp.float32), flags[0][a]
            )

    def settle():
        for load in small:
            load.wait()
        for core_side in (b, 1 - b):
            flags.append([is_active(core_side, a) for a in range(tiles)])
        for a in range(tiles):
            use_near.append(is_listed(a, b * tiles + 1 - a))
            use_last.append(is_listed(a, (1 - b) * tiles + 1))
        for load in loads[:2]:
            load.wait()
        for g in range(sets):
            pl.loop(0, GROUPED // PACK)(functools.partial(split_pair, g))
            for copy in kv_swap(g):
                copy.start()
        loads[2].wait()
        for own in owns:
            own.start()
        for load in loads[3:]:
            load.start()
        swap_in.start()

    def collect():
        @pl.loop(0, pieces)
        def _(n):
            _, beside, onward = a_copies(n)
            beside().wait_recv()
            onward().wait_recv()

        for load in loads[3:]:
            load.wait()
        swap_in.wait_recv()

    def drain_rest():
        swap_in.wait_send()
        for g in range(sets):
            for copy in kv_swap(g):
                copy.wait_send()

        @pl.loop(0, pieces)
        def _(n):
            for copy in a_copies(n):
                copy().wait_send()

    def drain(k):
        visit(k, 0, 0, done=True)
        if not z_first(k, 0):
            side(k, done=True)
        for u in (-1, 1, 2, 3):
            relay(k, u, done=True)

    share = pieces // sets
    steps = {
        "launch": launch,
        "settle": settle,
        "relay": relay,
        "side": side,
        "attend": attend_set,
        "forward": lambda g: pass_on(g * share, (g + 1) * share),
        "begin": begin,
        "far0": functools.partial(far_part, 0),
        "far1": functools.partial(far_part, 1),
        "near0": functools.partial(near_part, 0),
        "near1": functools.partial(near_part, 1),
        "take0": functools.partial(take, 0),
        "take1": functools.partial(take, 1),
        "drain": drain,
        "drain_rest": drain_rest,
    }
    collected = False
    for name, *details in ORDER:
        if name in ("begin", "far0") and not collected:
            collect()
            collected = True
        steps[name](*details)

    drained = [details[0] for name, *details in ORDER if name == "drain"]
    if ("drain_rest",) not in ORDER:
        drain_rest()
    for k in streams:
        if k not in drained:
            drain(k)
        for j in range(2):
            p_copy(k, j).wait_send()
        out_copy(k).wait()


def local_fused(
    count,
    block_input,
    gate,
    q_fresh,
    kv_fresh,
    kv_cache,
    active_list,
    active_count,
    key_list,
    out_weight,
):
    tok, width = block_input.shape
    rows = out_weight.shape[0]
    quarter = width // 4
    unit = quarter // UNITS
    columns = q_fresh.shape[1]
    heads = columns // HEAD_DIM
    sets = heads // GROUPED
    pieces = heads // PACK
    streams = len(STREAMS)
    anywhere = pl.BlockSpec(memory_space=pltpu.HBM)
    dma = pltpu.SemaphoreType.DMA

    def vmem(*shape):
        return pltpu.VMEM(shape, jnp.bfloat16)

    return pl.pallas_call(
        fused,
        out_shape=pltpu.VMEM((tok, width), jnp.bfloat16),
        in_specs=[anywhere] * 9,
        out_specs=pl.BlockSpec(memory_space=pltpu.VMEM),
        scratch_shapes=[
            [vmem(count * rows, size * unit) for _, size in STREAMS],
            vmem(tok, columns),
            vmem(tok, 2, columns),
            vmem(tok, 2, columns),
            pltpu.VMEM((PACK, 2 * tok, HEAD_DIM), jnp.float32),
            [vmem(2 * tok, GROUPED * HEAD_DIM) for _ in range(sets)],
            [vmem(2 * tok, GROUPED * HEAD_DIM) for _ in range(sets)],
            vmem(4 * tok, columns),
            vmem(tok, width),
            vmem(tok, quarter),
            vmem(tok, quarter),
            vmem(2 * tok, quarter),
            vmem(2 * tok, quarter),
            [
                pltpu.VMEM((2 * tok, STREAMS[details[0]][1] * unit), jnp.float32)
                for name, *details in ORDER
                if name == "begin"
            ],
            pltpu.VMEM((1, width), jnp.float32),
            pltpu.SMEM(active_list.shape, jnp.int32),
            pltpu.SMEM(active_count.shape, jnp.int32),
            pltpu.SMEM((key_list.shape[2],) + key_list.shape[:2], jnp.int32),
            dma((8,)),
            dma((streams,)),
            dma((streams, count, 3)),
            dma((streams, count)),
            dma((2, sets)),
            dma((2, sets)),
            dma((1,)),
            dma((1,)),
            dma((3, pieces)),
            dma((3, pieces)),
            dma((streams, 2)),
            dma((streams, 2)),
            dma((streams,)),
            dma((streams,)),
        ],
        compiler_params=pltpu.CompilerParams(
            collective_id=0, has_side_effects=True, vmem_limit_bytes=56000000
        ),
    )(
        active_list,
        active_count,
        key_list.transpose(2, 0, 1),
        block_input,
        gate[None, :],
        q_fresh,
        kv_fresh,
        kv_cache,
        out_weight,
    )


def per_device(groups, count, cores, *args):
    rows, width = args[-1].shape
    columns = args[2].shape[1]
    fits = groups == 2 and cores == 2 and count == DEPTH * LINE and rows % 16 == 0
    fits = fits and width % (4 * UNITS * 128) == 0 and count * rows * width < 1 << 24
    fits = fits and columns % (GROUPED * HEAD_DIM) == 0 and LINE * rows % 128 == 0
    fits = fits and args[5].shape[2] == 2 and args[7].shape[1:] == (4, 3)
    return local_fused(count, *args) if fits else local(*args)


def solution(mesh):
    in_specs = (
        P(("groups", "fsdp", "blk"), None),
        P("groups"),
        P(("groups", "fsdp", "blk"), None),
        P(("groups", "fsdp", "blk"), None, None),
        P(("groups", "fsdp", "blk"), None, None),
        P(("groups", "fsdp"), None, None),
        P(("groups", "fsdp"), None),
        P(("groups", "fsdp"), None, None),
        P("fsdp", None),
    )
    sizes = [mesh.shape[axis] for axis in ("groups", "fsdp", "blk")]
    body = functools.partial(per_device, *sizes)
    out_specs = P(("groups", "fsdp", "blk"), None)
    return jax.shard_map(body, mesh=mesh, in_specs=in_specs, out_specs=out_specs, check_vma=False)
```

```python
import functools
import math

import jax
import jax.numpy as jnp
from jax import lax
from jax.experimental import pallas as pl
from jax.experimental.pallas import tpu as pltpu
from jax.sharding import PartitionSpec as P

HEADS = 20
HEAD_DIM = 128


MASKED = -1e30


def swapped(block, axis, apart):
    count = lax.axis_size(axis)
    route = []
    for low in range(count):
        high = low | 1 << apart
        if high != low and high < count:
            route += [(low, high), (high, low)]
    return lax.ppermute(block, axis, route)


def tile_flags(tile_list, tile_count):
    slot_ids = jnp.arange(tile_list.shape[0], dtype=jnp.int32)
    listed = (tile_list[:, None] == slot_ids[None, :]) & (slot_ids[:, None] < tile_count)
    return jnp.any(listed, axis=0)


def block_partial(query_tile, key_rows, value_rows, allowed):
    tile_rows = query_tile.shape[0]
    query3 = query_tile.reshape(tile_rows, HEADS, HEAD_DIM)
    key3 = key_rows.reshape(key_rows.shape[0], HEADS, HEAD_DIM)
    value3 = value_rows.reshape(value_rows.shape[0], HEADS, HEAD_DIM)
    scores = jnp.einsum(
        "qhd,khd->hqk", query3, key3, preferred_element_type=jnp.float32
    ) / math.sqrt(HEAD_DIM)
    scores = jnp.where(allowed[None, None, :], scores, MASKED)
    row_max = jnp.max(scores, axis=2)
    exp_terms = jnp.where(allowed[None, None, :], jnp.exp(scores - row_max[:, :, None]), 0.0)
    row_total = jnp.sum(exp_terms, axis=2)
    weights = exp_terms.astype(jnp.bfloat16)
    block_out = jnp.einsum("hqk,khd->hqd", weights, value3, preferred_element_type=jnp.float32)
    return (block_out, row_max, row_total)


def attend_block(
    queries, tile_list, tile_count, query_side, key_rows, value_rows, key_side, key_table
):
    tiles_dev = tile_list.shape[0]
    tile_rows = queries.shape[0] // tiles_dev
    slot_ids = jnp.arange(tiles_dev, dtype=jnp.int32)
    key_tiles = key_side * tiles_dev + slot_ids
    init_state = (
        jnp.zeros((tiles_dev, HEADS, tile_rows, HEAD_DIM), jnp.float32),
        jnp.full((tiles_dev, HEADS, tile_rows), MASKED, jnp.float32),
        jnp.zeros((tiles_dev, HEADS, tile_rows), jnp.float32),
    )

    def one_slot(slot_idx, carry_state):
        tile_pos = tile_list[slot_idx]
        query_tile = lax.dynamic_slice_in_dim(queries, tile_pos * tile_rows, tile_rows, 0)
        listed = key_table[query_side * tiles_dev + tile_pos]
        allowed_tiles = jnp.any(key_tiles[:, None] == listed[None, :], axis=1)
        allowed = jnp.repeat(allowed_tiles, tile_rows, total_repeat_length=tiles_dev * tile_rows)
        partial_value = block_partial(query_tile, key_rows, value_rows, allowed)
        return tuple(
            (whole.at[tile_pos].set(piece) for whole, piece in zip(carry_state, partial_value))
        )

    return lax.fori_loop(0, tile_count, one_slot, init_state)


def merge_states(earlier, later_state):
    out_one, max_one, total_one = earlier
    out_two, max_two, total_two = later_state
    joint_max = jnp.maximum(max_one, max_two)
    scale_one = jnp.exp(max_one - joint_max)
    scale_two = jnp.exp(max_two - joint_max)
    summed = out_one * scale_one[..., None] + out_two * scale_two[..., None]
    return (summed, total_one * scale_one + total_two * scale_two)


def local(
    block_input, gate, q_fresh, kv_fresh, kv_cache, active_list, active_count, key_list, out_weight
):
    own_side = lax.axis_index("blk")
    other_side = 1 - own_side
    tiles_dev = active_list.shape[2]
    tok_dev = block_input.shape[0]
    tile_rows = tok_dev // tiles_dev
    own_list = active_list[0, own_side]
    own_count = active_count[0, own_side]
    flags = tile_flags(own_list, own_count)
    row_flags = jnp.repeat(flags, tile_rows, total_repeat_length=tok_dev)
    resident = jnp.where(row_flags[:, None, None], kv_fresh, kv_cache)
    key_table = key_list[0]
    own_state = attend_block(
        q_fresh, own_list, own_count, own_side, resident[:, 0], resident[:, 1], own_side, key_table
    )
    other_kv = swapped(resident, "blk", 0)
    other_state = attend_block(
        q_fresh,
        own_list,
        own_count,
        own_side,
        other_kv[:, 0],
        other_kv[:, 1],
        other_side,
        key_table,
    )
    summed, denom = merge_states(own_state, other_state)
    denom = jnp.where(flags[:, None, None], denom, 1.0)
    attended = (
        (summed / denom[..., None])
        .transpose(0, 2, 1, 3)
        .reshape(tok_dev, HEADS * HEAD_DIM)
        .astype(jnp.bfloat16)
    )
    half_cols = out_weight.shape[1] // 2
    own_cols = lax.dynamic_slice_in_dim(out_weight, own_side * half_cols, half_cols, 1)
    half_weight = lax.all_gather(own_cols, "fsdp", axis=0, tiled=True)
    partner_rows = swapped(attended, "blk", 0)
    own_part = jnp.dot(attended, half_weight, preferred_element_type=jnp.float32)
    partner_part = jnp.dot(partner_rows, half_weight, preferred_element_type=jnp.float32)
    returned = swapped(partner_part, "blk", 0)
    projected = jnp.where(
        own_side == 0,
        jnp.concatenate([own_part, returned], axis=1),
        jnp.concatenate([returned, own_part], axis=1),
    )
    mixed = block_input.astype(jnp.float32) + gate[None, :] * projected
    return jnp.where(row_flags[:, None], mixed.astype(jnp.bfloat16), block_input)


MESH = pl.DeviceIdType.MESH
LINE = 2
DEPTH = 4
LONG, MIXED, SHORT = range(3)
STREAMS = ((LONG, 2), (LONG, 2), (LONG, 2), (LONG, 1), (LONG, 1), (SHORT, 1), (SHORT, 1))
UNITS = sum(size for _, size in STREAMS)
PACK = 2
GROUPED = 4
ORDER = (
    ("launch", 0), ("launch", 5), ("launch", 4), ("launch", 1), ("settle",), ("attend", 0),
    ("relay", 0, 1), ("attend", 1), ("relay", 1, -1), ("relay", 4, -1), ("relay", 4, 1),
    ("relay", 1, 1), ("launch", 2), ("forward", 0), ("relay", 0, -1), ("side", 5),
    ("attend", 2), ("relay", 4, 2), ("relay", 1, 2), ("forward", 1), ("attend", 3),
    ("relay", 0, 2), ("relay", 4, 3), ("relay", 5, 1), ("forward", 2), ("attend", 4),
    ("forward", 3), ("relay", 1, 3), ("relay", 0, 3), ("relay", 2, 1), ("launch", 6),
    ("relay", 2, -1), ("forward", 4), ("far0", 1), ("far0", 4), ("relay", 5, -1),
    ("relay", 2, 2), ("near0", 1), ("far0", 0), ("near1", 0), ("far1", 1), ("launch", 3),
    ("near0", 0), ("far1", 4), ("relay", 5, 2), ("relay", 2, 3), ("take0", 4), ("far1", 0),
    ("side", 6), ("begin", 5), ("relay", 3, -1), ("near1", 1), ("relay", 5, 3), ("take0", 1),
    ("far0", 5), ("relay", 3, 1), ("take0", 0), ("near0", 4), ("far1", 5), ("near1", 5),
    ("near0", 5), ("relay", 3, 2), ("far0", 2), ("relay", 3, 3), ("relay", 6, -1),
    ("relay", 6, 1), ("take1", 4), ("far1", 2), ("take1", 0), ("near0", 2), ("near1", 2),
    ("take1", 5), ("relay", 6, 2), ("far0", 3), ("far1", 3), ("begin", 6), ("near1", 3),
    ("near0", 3), ("drain_rest",), ("drain", 0), ("drain", 1), ("drain", 2), ("relay", 6, 3),
    ("far0", 6), ("near0", 6), ("take1", 1), ("far1", 6), ("near1", 4), ("take1", 3),
    ("take1", 2), ("near1", 6), ("take0", 3), ("take0", 2), ("take0", 6), ("drain", 3),
    ("drain", 4), ("drain", 5), ("drain", 6), ("take0", 5), ("take1", 6),
)


def fused(
    list_hbm,
    count_hbm,
    keys_hbm,
    block_hbm,
    gate_hbm,
    q_hbm,
    fresh_hbm,
    cache_hbm,
    w_hbm,
    out_ref,
    weights,
    queries,
    fresh,
    cache,
    wide,
    keys,
    values,
    attended,
    mixed_in,
    pair_in,
    pair_out,
    sent,
    received,
    sums,
    gate_ref,
    active_list,
    active_count,
    key_list,
    load_sem,
    own_sem,
    w_send,
    w_recv,
    kv_send,
    kv_recv,
    in_send,
    in_recv,
    a_send,
    a_recv,
    p_send,
    p_recv,
    out_send,
    out_recv,
    diagonal,
):
    me = lax.axis_index("fsdp")
    z, x = me // LINE, me % LINE
    y = lax.axis_index("groups")
    b = lax.axis_index("blk")
    rows = w_hbm.shape[0]
    tok = q_hbm.shape[0]
    quarter = w_hbm.shape[1] // 4
    unit = quarter // UNITS
    tiles = active_list.shape[2]
    tile_rows = tok // tiles
    heads = q_hbm.shape[1] // HEAD_DIM
    sets = heads // GROUPED
    piece = PACK * HEAD_DIM
    pieces = heads // PACK
    listed = key_list.shape[0]

    def quarter_of(group, core):
        return pl.multiple_of((2 * group + core) * quarter, 128)

    mine = quarter_of(y, b)

    barrier = pltpu.get_barrier_semaphore()
    inward = jnp.where(z < DEPTH // 2, 1, -1)
    inner = (z > 0) & (z < DEPTH - 1)
    at_end = (z == 0) | (z == DEPTH - 1)
    targets = (
        (None, {"fsdp": me + inward * LINE}),
        (inner, {"fsdp": me - inward * LINE}),
        (None, {"fsdp": z * LINE + 1 - x}),
    )
    twin = {"groups": 1 - y}
    core = {"blk": 1 - b}
    cross = {"groups": 1 - y, "blk": 1 - b}

    def when(cond, body):
        if cond is None:
            body()
        else:
            pl.when(cond)(body)

    def greet(device):
        pl.semaphore_signal(barrier, inc=1, device_id=device, device_id_type=MESH)

    for cond, device in ((None, twin),) + targets + ((None, core),):
        when(cond, functools.partial(greet, device))

    def remote(src, dst, send, recv, device):
        return pltpu.make_async_remote_copy(
            src_ref=src,
            dst_ref=dst,
            send_sem=send,
            recv_sem=recv,
            device_id=device,
            device_id_type=MESH,
        )

    def extent(k):
        return sum(size for _, size in STREAMS[:k]) * unit, STREAMS[k][1] * unit

    def shard(k, s):
        return weights[k].at[pl.ds(pl.multiple_of(s * rows, 16), rows), :]

    def own_cols(k):
        low, size = extent(k)
        return w_hbm.at[:, pl.ds(pl.multiple_of(mine + low, 128), size)]

    streams = range(len(STREAMS))

    loads = [
        pltpu.make_async_copy(fresh_hbm, fresh, load_sem.at[0]),
        pltpu.make_async_copy(cache_hbm, cache, load_sem.at[1]),
        pltpu.make_async_copy(q_hbm, queries, load_sem.at[2]),
        pltpu.make_async_copy(block_hbm, mixed_in, load_sem.at[3]),
        pltpu.make_async_copy(gate_hbm, gate_ref, load_sem.at[4]),
    ]
    small = [
        pltpu.make_async_copy(list_hbm, active_list, load_sem.at[5]),
        pltpu.make_async_copy(count_hbm, active_count, load_sem.at[6]),
        pltpu.make_async_copy(keys_hbm, key_list, load_sem.at[7]),
    ]
    owns = [pltpu.make_async_copy(own_cols(k), shard(k, me), own_sem.at[k]) for k in streams]
    for load in loads[:3] + small:
        load.start()

    pl.semaphore_wait(barrier, 4 + inner.astype(jnp.int32))
    pl.semaphore_signal(diagonal, inc=1, device_id=core, device_id_type=MESH)

    swap_in = remote(
        block_hbm.at[:, pl.ds(quarter_of(y, 1 - b), quarter)],
        pair_in,
        in_send.at[0],
        in_recv.at[0],
        core,
    )

    def shard_copy(k, s, way, own=False):
        return remote(
            own_cols(k) if own else shard(k, s),
            shard(k, s),
            w_send.at[k, s, way],
            w_recv.at[k, s],
            targets[way][1],
        )

    def z_first(k, u):
        kind = STREAMS[k][0]
        return kind == LONG or (kind == MIXED and u == 3)

    places = {0: None, -1: inner, 1: None, 2: None, 3: at_end}

    def ways_of(k, u, dx):
        onward = dx == 0 or not (z_first(k, u) or (STREAMS[k][0] == MIXED and u == 2))
        found = []
        if onward and u in (0, -1):
            found.append(0)
        if onward and u in (0, 1, 2):
            found.append(1)
        if dx == 0 and (u == 0 or z_first(k, u)):
            found.append(2)
        return found

    def visit(k, u, dx, done=False):
        s = (z + inward * u) * LINE + (x if dx == 0 else 1 - x)
        own = (u, dx) == (0, 0)

        def body():
            if not done and not own:
                shard_copy(k, s, 2).wait_recv()

            def act(way):
                copy = shard_copy(k, s, way, own)
                if done:
                    copy.wait_send()
                else:
                    copy.start()

            for way in ways_of(k, u, dx):
                when(targets[way][0], functools.partial(act, way))

        when(places[u], body)

    def launch(k):
        visit(k, 0, 0)

    def relay(k, u, done=False):
        visit(k, u, 0, done)
        if not z_first(k, u):
            visit(k, u, 1, done)

    def side(k, done=False):
        visit(k, 0, 1, done)

    def arrive(k):
        def wait(u):
            s = (z + inward * u) * LINE + 1 - x
            shard_copy(k, s, 2).wait_recv()

        for u in (0, -1, 1, 2, 3):
            if z_first(k, u):
                when(places[u], functools.partial(wait, u))

    def is_active(core_side, a):
        found = jnp.int32(0)
        for slot in range(tiles):
            hit = (active_list[0, core_side, slot] == a) & (slot < active_count[0, core_side])
            found = jnp.where(hit, jnp.int32(1), found)
        return found

    flags = []

    whole = pl.ds(pl.multiple_of(b * tok, 16), tok)

    def split_pair(g, i):
        for k in range(PACK):
            local_col = pl.multiple_of((i * PACK + k) * HEAD_DIM, 128)
            local_cols = pl.ds(local_col, HEAD_DIM)
            cols = pl.ds(pl.multiple_of(g * GROUPED * HEAD_DIM + local_col, 128), HEAD_DIM)
            for a in range(tiles):
                span = pl.ds(a * tile_rows, tile_rows)
                pair = jnp.where(flags[0][a] > 0, fresh[span, :, cols], cache[span, :, cols])
                pair = pair.reshape(2 * tile_rows, HEAD_DIM)
                wide[k, pl.ds(2 * a * tile_rows, 2 * tile_rows), :] = pair.astype(jnp.float32)
            keys[g][whole, local_cols] = wide[k, pl.ds(0, tok, 2), :].astype(jnp.bfloat16)
            values[g][whole, local_cols] = wide[k, pl.ds(1, tok, 2), :].astype(jnp.bfloat16)

    def kv_swap(g):
        return [
            remote(
                ref.at[whole, :], ref.at[whole, :], kv_send.at[j, g], kv_recv.at[j, g], core
            )
            for j, ref in enumerate((keys[g], values[g]))
        ]

    def is_listed(a, tile):
        found = jnp.int32(0)
        for t in range(listed):
            found = jnp.where(key_list[t, 0, b * tiles + a] == tile, jnp.int32(1), found)
        return found

    def tile_span(core_side, a):
        return pl.ds(pl.multiple_of(core_side * tok + a * tile_rows, 16), tile_rows)

    first_far, last_far = tile_span(1 - b, 0), tile_span(1 - b, 1)
    use_near, use_last = [], []

    def three_tiles(ref, cols, a):
        spare = ref[first_far, cols]
        second = jnp.where(use_near[a] > 0, ref[tile_span(b, 1 - a), cols], spare)
        third = jnp.where(use_last[a] > 0, ref[last_far, cols], spare)
        return jnp.concatenate([ref[tile_span(b, a), cols], second, third], axis=0)

    factor = math.log2(math.e) / math.sqrt(HEAD_DIM)

    def rows_of(slot):
        return pl.ds(slot * tok, tok)

    def a_copies(n):
        cols = pl.ds(pl.multiple_of(n * piece, 128), piece)
        own = attended.at[rows_of(0), cols]
        over = attended.at[rows_of(2), cols]
        beside = attended.at[rows_of(1), cols]
        onward = attended.at[rows_of(3), cols]

        def lazy(j, src, dst, device):
            return lambda: remote(src, dst, a_send.at[j, n], a_recv.at[j, n], device)

        return lazy(0, own, over, twin), lazy(1, own, beside, core), lazy(2, over, onward, core)

    def attend(g, i):
        for k in range(PACK):
            local_col = pl.multiple_of((i * PACK + k) * HEAD_DIM, 128)
            local_cols = pl.ds(local_col, HEAD_DIM)
            cols = pl.ds(pl.multiple_of(g * GROUPED * HEAD_DIM + local_col, 128), HEAD_DIM)
            for a in range(tiles):
                query = queries[pl.ds(a * tile_rows, tile_rows), cols]
                key_rows = three_tiles(keys[g], local_cols, a)
                value_rows = three_tiles(values[g], local_cols, a)
                scores = lax.dot_general(
                    query, key_rows, (((1,), (1,)), ((), ())), preferred_element_type=jnp.float32
                )
                top = jnp.max(scores, axis=1, keepdims=True)
                terms = jnp.exp2((scores - top) * factor)
                total = jnp.sum(terms, axis=1, keepdims=True)
                summed = jnp.dot(
                    terms.astype(jnp.bfloat16), value_rows, preferred_element_type=jnp.float32
                )
                attended[pl.ds(a * tile_rows, tile_rows), cols] = (summed / total).astype(
                    jnp.bfloat16
                )
        n = g * (GROUPED // PACK) + i
        over, beside, _ = a_copies(n)
        over().start()
        beside().start()

    def attend_set(g):
        for copy in kv_swap(g):
            copy.wait_recv()
        pl.loop(0, GROUPED // PACK)(functools.partial(attend, g))

    def pass_on(low, high):
        @pl.loop(low, high)
        def _(n):
            over, _, onward = a_copies(n)
            over().wait_recv()
            onward().start()

    def p_copy(k, j):
        low, size = extent(k)
        part = (pl.ds(j * tok, tok), pl.ds(low, size))
        return remote(
            sent.at[part], received.at[part], p_send.at[k, j], p_recv.at[k, j], (cross, twin)[j]
        )

    def out_copy(k):
        low, size = extent(k)
        return remote(
            pair_out.at[:, pl.ds(low, size)],
            out_ref.at[:, pl.ds(pl.multiple_of(mine + low, 128), size)],
            out_send.at[k],
            out_recv.at[k],
            core,
        )

    span_rows = LINE * rows
    last_start = pl.multiple_of(jnp.where(z < DEPTH // 2, (DEPTH - 1) * span_rows, 0), 128)
    first_start = pl.multiple_of(jnp.where(z < DEPTH // 2, 0, span_rows), 128)
    begun = [details[0] for name, *details in ORDER if name == "begin"]
    early = dict(zip(begun, sums))

    def product(slot, k, start=None, depth=None):
        if depth is None:
            left, right = attended[rows_of(slot), :], weights[k][...]
        else:
            inner_span = pl.ds(start, depth)
            left, right = attended[rows_of(slot), inner_span], weights[k][inner_span, :]
        return jnp.dot(left, right, preferred_element_type=jnp.float32)

    def far_part(j, k):
        if j == 0:
            arrive(k)
            if k not in early:
                owns[k].wait()
        low, size = extent(k)
        if k in early:
            part = early[k][pl.ds(j * tok, tok), :] + product(3 - j, k, last_start, span_rows)
        else:
            part = product(3 - j, k)
        sent[pl.ds(j * tok, tok), pl.ds(low, size)] = part.astype(jnp.bfloat16)
        p_copy(k, j).start()

    def begin(k):
        owns[k].wait()
        for j in range(2):
            part = product(3 - j, k, first_start, (DEPTH - 1) * span_rows)
            early[k][pl.ds(j * tok, tok), :] = part

    def blend(before, gate, part, flag):
        before = before.astype(jnp.float32)
        return jnp.where(flag > 0, before + gate * part, before).astype(jnp.bfloat16)

    def near_part(j, k):
        low, size = extent(k)
        cols = pl.ds(pl.multiple_of(mine + low, 128), size)
        local_cols = pl.ds(low, size)
        gate = gate_ref[:, cols]
        part = product(1 - j, k)
        for a in range(tiles):
            span = pl.ds(a * tile_rows, tile_rows)
            term = part[a * tile_rows : (a + 1) * tile_rows]
            if j == 0:
                pair_out[span, local_cols] = blend(
                    pair_in[span, local_cols], gate, term, flags[1][a]
                )
            else:
                out_ref[span, cols] = blend(mixed_in[span, cols], gate, term, flags[0][a])
        if j == 0:
            out_copy(k).start()

    def take(j, k):
        low, size = extent(k)
        p_copy(k, j).wait_recv()
        base = quarter_of(1 - y, b if j == 1 else 1 - b)
        cols = pl.ds(pl.multiple_of(base + low, 128), size)
        gate = gate_ref[:, cols]
        for a in range(tiles):
            span = pl.ds(a * tile_rows, tile_rows)
            part = received[pl.ds(j * tok + a * tile_rows, tile_rows), pl.ds(low, size)]
            out_ref[span, cols] = blend(
                mixed_in[span, cols], gate, part.astype(jnp.float32), flags[0][a]
            )

    def settle():
        for load in small:
            load.wait()
        for core_side in (b, 1 - b):
            flags.append([is_active(core_side, a) for a in range(tiles)])
        for a in range(tiles):
            use_near.append(is_listed(a, b * tiles + 1 - a))
            use_last.append(is_listed(a, (1 - b) * tiles + 1))
        for load in loads[:2]:
            load.wait()
        for g in range(sets):
            pl.loop(0, GROUPED // PACK)(functools.partial(split_pair, g))
            for copy in kv_swap(g):
                copy.start()
        loads[2].wait()
        for own in owns:
            own.start()
        for load in loads[3:]:
            load.start()
        swap_in.start()

    def collect():
        @pl.loop(0, pieces)
        def _(n):
            _, beside, onward = a_copies(n)
            beside().wait_recv()
            onward().wait_recv()

        for load in loads[3:]:
            load.wait()
        swap_in.wait_recv()
        pl.semaphore_wait(diagonal, 1)

    def drain_rest():
        swap_in.wait_send()
        for g in range(sets):
            for copy in kv_swap(g):
                copy.wait_send()

        @pl.loop(0, pieces)
        def _(n):
            for copy in a_copies(n):
                copy().wait_send()

    def drain(k):
        visit(k, 0, 0, done=True)
        if not z_first(k, 0):
            side(k, done=True)
        for u in (-1, 1, 2, 3):
            relay(k, u, done=True)

    share = pieces // sets
    steps = {
        "launch": launch,
        "settle": settle,
        "relay": relay,
        "side": side,
        "attend": attend_set,
        "forward": lambda g: pass_on(g * share, (g + 1) * share),
        "begin": begin,
        "far0": functools.partial(far_part, 0),
        "far1": functools.partial(far_part, 1),
        "near0": functools.partial(near_part, 0),
        "near1": functools.partial(near_part, 1),
        "take0": functools.partial(take, 0),
        "take1": functools.partial(take, 1),
        "drain": drain,
        "drain_rest": drain_rest,
    }
    collected = False
    for name, *details in ORDER:
        if name in ("begin", "far0") and not collected:
            collect()
            collected = True
        steps[name](*details)

    drained = [details[0] for name, *details in ORDER if name == "drain"]
    if ("drain_rest",) not in ORDER:
        drain_rest()
    for k in streams:
        if k not in drained:
            drain(k)
        for j in range(2):
            p_copy(k, j).wait_send()
        out_copy(k).wait()


def local_fused(
    count,
    block_input,
    gate,
    q_fresh,
    kv_fresh,
    kv_cache,
    active_list,
    active_count,
    key_list,
    out_weight,
):
    tok, width = block_input.shape
    rows = out_weight.shape[0]
    quarter = width // 4
    unit = quarter // UNITS
    columns = q_fresh.shape[1]
    heads = columns // HEAD_DIM
    sets = heads // GROUPED
    pieces = heads // PACK
    streams = len(STREAMS)
    anywhere = pl.BlockSpec(memory_space=pltpu.HBM)
    dma = pltpu.SemaphoreType.DMA

    def vmem(*shape):
        return pltpu.VMEM(shape, jnp.bfloat16)

    return pl.pallas_call(
        fused,
        out_shape=pltpu.VMEM((tok, width), jnp.bfloat16),
        in_specs=[anywhere] * 9,
        out_specs=pl.BlockSpec(memory_space=pltpu.VMEM),
        scratch_shapes=[
            [vmem(count * rows, size * unit) for _, size in STREAMS],
            vmem(tok, columns),
            vmem(tok, 2, columns),
            vmem(tok, 2, columns),
            pltpu.VMEM((PACK, 2 * tok, HEAD_DIM), jnp.float32),
            [vmem(2 * tok, GROUPED * HEAD_DIM) for _ in range(sets)],
            [vmem(2 * tok, GROUPED * HEAD_DIM) for _ in range(sets)],
            vmem(4 * tok, columns),
            vmem(tok, width),
            vmem(tok, quarter),
            vmem(tok, quarter),
            vmem(2 * tok, quarter),
            vmem(2 * tok, quarter),
            [
                pltpu.VMEM((2 * tok, STREAMS[details[0]][1] * unit), jnp.float32)
                for name, *details in ORDER
                if name == "begin"
            ],
            pltpu.VMEM((1, width), jnp.float32),
            pltpu.SMEM(active_list.shape, jnp.int32),
            pltpu.SMEM(active_count.shape, jnp.int32),
            pltpu.SMEM((key_list.shape[2],) + key_list.shape[:2], jnp.int32),
            dma((8,)),
            dma((streams,)),
            dma((streams, count, 3)),
            dma((streams, count)),
            dma((2, sets)),
            dma((2, sets)),
            dma((1,)),
            dma((1,)),
            dma((3, pieces)),
            dma((3, pieces)),
            dma((streams, 2)),
            dma((streams, 2)),
            dma((streams,)),
            dma((streams,)),
            pltpu.SemaphoreType.REGULAR,
        ],
        compiler_params=pltpu.CompilerParams(
            collective_id=0, has_side_effects=True, vmem_limit_bytes=56000000
        ),
    )(
        active_list,
        active_count,
        key_list.transpose(2, 0, 1),
        block_input,
        gate[None, :],
        q_fresh,
        kv_fresh,
        kv_cache,
        out_weight,
    )


def per_device(groups, count, cores, *args):
    rows, width = args[-1].shape
    columns = args[2].shape[1]
    fits = groups == 2 and cores == 2 and count == DEPTH * LINE and rows % 16 == 0
    fits = fits and width % (4 * UNITS * 128) == 0 and count * rows * width < 1 << 24
    fits = fits and columns % (GROUPED * HEAD_DIM) == 0 and LINE * rows % 128 == 0
    fits = fits and args[5].shape[2] == 2 and args[7].shape[1:] == (4, 3)
    return local_fused(count, *args) if fits else local(*args)


def solution(mesh):
    in_specs = (
        P(("groups", "fsdp", "blk"), None),
        P("groups"),
        P(("groups", "fsdp", "blk"), None),
        P(("groups", "fsdp", "blk"), None, None),
        P(("groups", "fsdp", "blk"), None, None),
        P(("groups", "fsdp"), None, None),
        P(("groups", "fsdp"), None),
        P(("groups", "fsdp"), None, None),
        P("fsdp", None),
    )
    sizes = [mesh.shape[axis] for axis in ("groups", "fsdp", "blk")]
    body = functools.partial(per_device, *sizes)
    out_specs = P(("groups", "fsdp", "blk"), None)
    return jax.shard_map(body, mesh=mesh, in_specs=in_specs, out_specs=out_specs, check_vma=False)
```

```python
import functools
import math

import jax
import jax.numpy as jnp
from jax import lax
from jax.experimental import pallas as pl
from jax.experimental.pallas import tpu as pltpu
from jax.sharding import PartitionSpec as P

HEADS = 20
HEAD_DIM = 128


MASKED = -1e30


def swapped(block, axis, apart):
    count = lax.axis_size(axis)
    route = []
    for low in range(count):
        high = low | 1 << apart
        if high != low and high < count:
            route += [(low, high), (high, low)]
    return lax.ppermute(block, axis, route)


def tile_flags(tile_list, tile_count):
    slot_ids = jnp.arange(tile_list.shape[0], dtype=jnp.int32)
    listed = (tile_list[:, None] == slot_ids[None, :]) & (slot_ids[:, None] < tile_count)
    return jnp.any(listed, axis=0)


def block_partial(query_tile, key_rows, value_rows, allowed):
    tile_rows = query_tile.shape[0]
    query3 = query_tile.reshape(tile_rows, HEADS, HEAD_DIM)
    key3 = key_rows.reshape(key_rows.shape[0], HEADS, HEAD_DIM)
    value3 = value_rows.reshape(value_rows.shape[0], HEADS, HEAD_DIM)
    scores = jnp.einsum(
        "qhd,khd->hqk", query3, key3, preferred_element_type=jnp.float32
    ) / math.sqrt(HEAD_DIM)
    scores = jnp.where(allowed[None, None, :], scores, MASKED)
    row_max = jnp.max(scores, axis=2)
    exp_terms = jnp.where(allowed[None, None, :], jnp.exp(scores - row_max[:, :, None]), 0.0)
    row_total = jnp.sum(exp_terms, axis=2)
    weights = exp_terms.astype(jnp.bfloat16)
    block_out = jnp.einsum("hqk,khd->hqd", weights, value3, preferred_element_type=jnp.float32)
    return (block_out, row_max, row_total)


def attend_block(
    queries, tile_list, tile_count, query_side, key_rows, value_rows, key_side, key_table
):
    tiles_dev = tile_list.shape[0]
    tile_rows = queries.shape[0] // tiles_dev
    slot_ids = jnp.arange(tiles_dev, dtype=jnp.int32)
    key_tiles = key_side * tiles_dev + slot_ids
    init_state = (
        jnp.zeros((tiles_dev, HEADS, tile_rows, HEAD_DIM), jnp.float32),
        jnp.full((tiles_dev, HEADS, tile_rows), MASKED, jnp.float32),
        jnp.zeros((tiles_dev, HEADS, tile_rows), jnp.float32),
    )

    def one_slot(slot_idx, carry_state):
        tile_pos = tile_list[slot_idx]
        query_tile = lax.dynamic_slice_in_dim(queries, tile_pos * tile_rows, tile_rows, 0)
        listed = key_table[query_side * tiles_dev + tile_pos]
        allowed_tiles = jnp.any(key_tiles[:, None] == listed[None, :], axis=1)
        allowed = jnp.repeat(allowed_tiles, tile_rows, total_repeat_length=tiles_dev * tile_rows)
        partial_value = block_partial(query_tile, key_rows, value_rows, allowed)
        return tuple(
            (whole.at[tile_pos].set(piece) for whole, piece in zip(carry_state, partial_value))
        )

    return lax.fori_loop(0, tile_count, one_slot, init_state)


def merge_states(earlier, later_state):
    out_one, max_one, total_one = earlier
    out_two, max_two, total_two = later_state
    joint_max = jnp.maximum(max_one, max_two)
    scale_one = jnp.exp(max_one - joint_max)
    scale_two = jnp.exp(max_two - joint_max)
    summed = out_one * scale_one[..., None] + out_two * scale_two[..., None]
    return (summed, total_one * scale_one + total_two * scale_two)


def local(
    block_input, gate, q_fresh, kv_fresh, kv_cache, active_list, active_count, key_list, out_weight
):
    own_side = lax.axis_index("blk")
    other_side = 1 - own_side
    tiles_dev = active_list.shape[2]
    tok_dev = block_input.shape[0]
    tile_rows = tok_dev // tiles_dev
    own_list = active_list[0, own_side]
    own_count = active_count[0, own_side]
    flags = tile_flags(own_list, own_count)
    row_flags = jnp.repeat(flags, tile_rows, total_repeat_length=tok_dev)
    resident = jnp.where(row_flags[:, None, None], kv_fresh, kv_cache)
    key_table = key_list[0]
    own_state = attend_block(
        q_fresh, own_list, own_count, own_side, resident[:, 0], resident[:, 1], own_side, key_table
    )
    other_kv = swapped(resident, "blk", 0)
    other_state = attend_block(
        q_fresh,
        own_list,
        own_count,
        own_side,
        other_kv[:, 0],
        other_kv[:, 1],
        other_side,
        key_table,
    )
    summed, denom = merge_states(own_state, other_state)
    denom = jnp.where(flags[:, None, None], denom, 1.0)
    attended = (
        (summed / denom[..., None])
        .transpose(0, 2, 1, 3)
        .reshape(tok_dev, HEADS * HEAD_DIM)
        .astype(jnp.bfloat16)
    )
    half_cols = out_weight.shape[1] // 2
    own_cols = lax.dynamic_slice_in_dim(out_weight, own_side * half_cols, half_cols, 1)
    half_weight = lax.all_gather(own_cols, "fsdp", axis=0, tiled=True)
    partner_rows = swapped(attended, "blk", 0)
    own_part = jnp.dot(attended, half_weight, preferred_element_type=jnp.float32)
    partner_part = jnp.dot(partner_rows, half_weight, preferred_element_type=jnp.float32)
    returned = swapped(partner_part, "blk", 0)
    projected = jnp.where(
        own_side == 0,
        jnp.concatenate([own_part, returned], axis=1),
        jnp.concatenate([returned, own_part], axis=1),
    )
    mixed = block_input.astype(jnp.float32) + gate[None, :] * projected
    return jnp.where(row_flags[:, None], mixed.astype(jnp.bfloat16), block_input)


MESH = pl.DeviceIdType.MESH
LINE = 2
DEPTH = 4
LONG, MIXED, SHORT = range(3)
STREAMS = ((LONG, 2), (LONG, 2), (LONG, 2), (LONG, 1), (LONG, 1), (SHORT, 1), (SHORT, 1))
UNITS = sum(size for _, size in STREAMS)
PACK = 2
GROUPED = 4
ORDER = (
    ("launch", 0), ("launch", 5), ("launch", 4), ("launch", 1), ("settle",), ("attend", 0),
    ("relay", 0, 1), ("attend", 1), ("relay", 1, -1), ("relay", 4, -1), ("relay", 4, 1),
    ("relay", 1, 1), ("launch", 2), ("forward", 0), ("relay", 0, -1), ("side", 5),
    ("attend", 2), ("relay", 4, 2), ("relay", 1, 2), ("forward", 1), ("attend", 3),
    ("relay", 0, 2), ("relay", 4, 3), ("relay", 5, 1), ("forward", 2), ("attend", 4),
    ("forward", 3), ("relay", 1, 3), ("relay", 0, 3), ("relay", 2, 1), ("launch", 6),
    ("relay", 2, -1), ("forward", 4), ("far0", 1), ("far0", 4), ("relay", 5, -1),
    ("relay", 2, 2), ("near0", 1), ("far0", 0), ("near1", 0), ("far1", 1), ("launch", 3),
    ("near0", 0), ("far1", 4), ("relay", 5, 2), ("relay", 2, 3), ("take0", 4), ("far1", 0),
    ("side", 6), ("begin", 5), ("relay", 3, -1), ("near1", 1), ("relay", 5, 3), ("take0", 1),
    ("far0", 5), ("relay", 3, 1), ("take0", 0), ("near0", 4), ("far1", 5), ("near1", 5),
    ("near0", 5), ("relay", 3, 2), ("far0", 2), ("relay", 3, 3), ("relay", 6, -1),
    ("relay", 6, 1), ("take1", 4), ("far1", 2), ("take1", 0), ("near0", 2), ("near1", 2),
    ("take1", 5), ("relay", 6, 2), ("far0", 3), ("far1", 3), ("begin", 6), ("near1", 3),
    ("near0", 3), ("drain_rest",), ("drain", 0), ("drain", 1), ("drain", 2), ("drain", 3),
    ("relay", 6, 3), ("far0", 6), ("near0", 6), ("take1", 1), ("far1", 6), ("near1", 4),
    ("take1", 3), ("take1", 2), ("near1", 6), ("take0", 3), ("take0", 2), ("take0", 6),
    ("drain", 4), ("drain", 5), ("drain", 6), ("take0", 5), ("take1", 6),
)


def fused(
    list_hbm,
    count_hbm,
    keys_hbm,
    block_hbm,
    gate_hbm,
    q_hbm,
    fresh_hbm,
    cache_hbm,
    w_hbm,
    out_ref,
    weights,
    queries,
    fresh,
    cache,
    wide,
    keys,
    values,
    attended,
    mixed_in,
    pair_in,
    pair_out,
    sent,
    received,
    sums,
    gate_ref,
    active_list,
    active_count,
    key_list,
    load_sem,
    own_sem,
    w_send,
    w_recv,
    kv_send,
    kv_recv,
    in_send,
    in_recv,
    a_send,
    a_recv,
    p_send,
    p_recv,
    out_send,
    out_recv,
    diagonal,
):
    me = lax.axis_index("fsdp")
    z, x = me // LINE, me % LINE
    y = lax.axis_index("groups")
    b = lax.axis_index("blk")
    rows = w_hbm.shape[0]
    tok = q_hbm.shape[0]
    quarter = w_hbm.shape[1] // 4
    unit = quarter // UNITS
    tiles = active_list.shape[2]
    tile_rows = tok // tiles
    heads = q_hbm.shape[1] // HEAD_DIM
    sets = heads // GROUPED
    piece = PACK * HEAD_DIM
    pieces = heads // PACK
    listed = key_list.shape[0]

    def quarter_of(group, core):
        return pl.multiple_of((2 * group + core) * quarter, 128)

    mine = quarter_of(y, b)

    barrier = pltpu.get_barrier_semaphore()
    inward = jnp.where(z < DEPTH // 2, 1, -1)
    inner = (z > 0) & (z < DEPTH - 1)
    at_end = (z == 0) | (z == DEPTH - 1)
    targets = (
        (None, {"fsdp": me + inward * LINE}),
        (inner, {"fsdp": me - inward * LINE}),
        (None, {"fsdp": z * LINE + 1 - x}),
    )
    twin = {"groups": 1 - y}
    core = {"blk": 1 - b}
    cross = {"groups": 1 - y, "blk": 1 - b}

    def when(cond, body):
        if cond is None:
            body()
        else:
            pl.when(cond)(body)

    def greet(device):
        pl.semaphore_signal(barrier, inc=1, device_id=device, device_id_type=MESH)

    for cond, device in ((None, twin),) + targets + ((None, core),):
        when(cond, functools.partial(greet, device))

    def remote(src, dst, send, recv, device):
        return pltpu.make_async_remote_copy(
            src_ref=src,
            dst_ref=dst,
            send_sem=send,
            recv_sem=recv,
            device_id=device,
            device_id_type=MESH,
        )

    def extent(k):
        return sum(size for _, size in STREAMS[:k]) * unit, STREAMS[k][1] * unit

    def shard(k, s):
        return weights[k].at[pl.ds(pl.multiple_of(s * rows, 16), rows), :]

    def own_cols(k):
        low, size = extent(k)
        return w_hbm.at[:, pl.ds(pl.multiple_of(mine + low, 128), size)]

    streams = range(len(STREAMS))

    loads = [
        pltpu.make_async_copy(fresh_hbm, fresh, load_sem.at[0]),
        pltpu.make_async_copy(cache_hbm, cache, load_sem.at[1]),
        pltpu.make_async_copy(q_hbm, queries, load_sem.at[2]),
        pltpu.make_async_copy(block_hbm, mixed_in, load_sem.at[3]),
        pltpu.make_async_copy(gate_hbm, gate_ref, load_sem.at[4]),
    ]
    small = [
        pltpu.make_async_copy(list_hbm, active_list, load_sem.at[5]),
        pltpu.make_async_copy(count_hbm, active_count, load_sem.at[6]),
        pltpu.make_async_copy(keys_hbm, key_list, load_sem.at[7]),
    ]
    owns = [pltpu.make_async_copy(own_cols(k), shard(k, me), own_sem.at[k]) for k in streams]
    for load in loads[:3] + small:
        load.start()

    pl.semaphore_wait(barrier, 4 + inner.astype(jnp.int32))
    pl.semaphore_signal(diagonal, inc=1, device_id=core, device_id_type=MESH)

    swap_in = remote(
        block_hbm.at[:, pl.ds(quarter_of(y, 1 - b), quarter)],
        pair_in,
        in_send.at[0],
        in_recv.at[0],
        core,
    )

    def shard_copy(k, s, way, own=False):
        return remote(
            own_cols(k) if own else shard(k, s),
            shard(k, s),
            w_send.at[k, s, way],
            w_recv.at[k, s],
            targets[way][1],
        )

    def z_first(k, u):
        kind = STREAMS[k][0]
        return kind == LONG or (kind == MIXED and u == 3)

    places = {0: None, -1: inner, 1: None, 2: None, 3: at_end}

    def ways_of(k, u, dx):
        onward = dx == 0 or not (z_first(k, u) or (STREAMS[k][0] == MIXED and u == 2))
        found = []
        if onward and u in (0, -1):
            found.append(0)
        if onward and u in (0, 1, 2):
            found.append(1)
        if dx == 0 and (u == 0 or z_first(k, u)):
            found.append(2)
        return found

    def visit(k, u, dx, done=False):
        s = (z + inward * u) * LINE + (x if dx == 0 else 1 - x)
        own = (u, dx) == (0, 0)

        def body():
            if not done and not own:
                shard_copy(k, s, 2).wait_recv()

            def act(way):
                copy = shard_copy(k, s, way, own)
                if done:
                    copy.wait_send()
                else:
                    copy.start()

            for way in ways_of(k, u, dx):
                when(targets[way][0], functools.partial(act, way))

        when(places[u], body)

    def launch(k):
        visit(k, 0, 0)

    def relay(k, u, done=False):
        visit(k, u, 0, done)
        if not z_first(k, u):
            visit(k, u, 1, done)

    def side(k, done=False):
        visit(k, 0, 1, done)

    def arrive(k):
        def wait(u):
            s = (z + inward * u) * LINE + 1 - x
            shard_copy(k, s, 2).wait_recv()

        for u in (0, -1, 1, 2, 3):
            if z_first(k, u):
                when(places[u], functools.partial(wait, u))

    def is_active(core_side, a):
        found = jnp.int32(0)
        for slot in range(tiles):
            hit = (active_list[0, core_side, slot] == a) & (slot < active_count[0, core_side])
            found = jnp.where(hit, jnp.int32(1), found)
        return found

    flags = []

    whole = pl.ds(pl.multiple_of(b * tok, 16), tok)

    def split_pair(g, i):
        for k in range(PACK):
            local_col = pl.multiple_of((i * PACK + k) * HEAD_DIM, 128)
            local_cols = pl.ds(local_col, HEAD_DIM)
            cols = pl.ds(pl.multiple_of(g * GROUPED * HEAD_DIM + local_col, 128), HEAD_DIM)
            for a in range(tiles):
                span = pl.ds(a * tile_rows, tile_rows)
                pair = jnp.where(flags[0][a] > 0, fresh[span, :, cols], cache[span, :, cols])
                pair = pair.reshape(2 * tile_rows, HEAD_DIM)
                wide[k, pl.ds(2 * a * tile_rows, 2 * tile_rows), :] = pair.astype(jnp.float32)
            keys[g][whole, local_cols] = wide[k, pl.ds(0, tok, 2), :].astype(jnp.bfloat16)
            values[g][whole, local_cols] = wide[k, pl.ds(1, tok, 2), :].astype(jnp.bfloat16)

    def kv_swap(g):
        return [
            remote(
                ref.at[whole, :], ref.at[whole, :], kv_send.at[j, g], kv_recv.at[j, g], core
            )
            for j, ref in enumerate((keys[g], values[g]))
        ]

    def is_listed(a, tile):
        found = jnp.int32(0)
        for t in range(listed):
            found = jnp.where(key_list[t, 0, b * tiles + a] == tile, jnp.int32(1), found)
        return found

    def tile_span(core_side, a):
        return pl.ds(pl.multiple_of(core_side * tok + a * tile_rows, 16), tile_rows)

    first_far, last_far = tile_span(1 - b, 0), tile_span(1 - b, 1)
    use_near, use_last = [], []

    def three_tiles(ref, cols, a):
        spare = ref[first_far, cols]
        second = jnp.where(use_near[a] > 0, ref[tile_span(b, 1 - a), cols], spare)
        third = jnp.where(use_last[a] > 0, ref[last_far, cols], spare)
        return jnp.concatenate([ref[tile_span(b, a), cols], second, third], axis=0)

    factor = math.log2(math.e) / math.sqrt(HEAD_DIM)

    def rows_of(slot):
        return pl.ds(slot * tok, tok)

    def a_copies(n):
        cols = pl.ds(pl.multiple_of(n * piece, 128), piece)
        own = attended.at[rows_of(0), cols]
        over = attended.at[rows_of(2), cols]
        beside = attended.at[rows_of(1), cols]
        onward = attended.at[rows_of(3), cols]

        def lazy(j, src, dst, device):
            return lambda: remote(src, dst, a_send.at[j, n], a_recv.at[j, n], device)

        return lazy(0, own, over, twin), lazy(1, own, beside, core), lazy(2, over, onward, core)

    def attend(g, i):
        for k in range(PACK):
            local_col = pl.multiple_of((i * PACK + k) * HEAD_DIM, 128)
            local_cols = pl.ds(local_col, HEAD_DIM)
            cols = pl.ds(pl.multiple_of(g * GROUPED * HEAD_DIM + local_col, 128), HEAD_DIM)
            for a in range(tiles):
                query = queries[pl.ds(a * tile_rows, tile_rows), cols]
                key_rows = three_tiles(keys[g], local_cols, a)
                value_rows = three_tiles(values[g], local_cols, a)
                scores = lax.dot_general(
                    query, key_rows, (((1,), (1,)), ((), ())), preferred_element_type=jnp.float32
                )
                top = jnp.max(scores, axis=1, keepdims=True)
                terms = jnp.exp2((scores - top) * factor)
                total = jnp.sum(terms, axis=1, keepdims=True)
                summed = jnp.dot(
                    terms.astype(jnp.bfloat16), value_rows, preferred_element_type=jnp.float32
                )
                attended[pl.ds(a * tile_rows, tile_rows), cols] = (summed / total).astype(
                    jnp.bfloat16
                )
        n = g * (GROUPED // PACK) + i
        over, beside, _ = a_copies(n)
        over().start()
        beside().start()

    def attend_set(g):
        for copy in kv_swap(g):
            copy.wait_recv()
        pl.loop(0, GROUPED // PACK)(functools.partial(attend, g))

    def pass_on(low, high):
        @pl.loop(low, high)
        def _(n):
            over, _, onward = a_copies(n)
            over().wait_recv()
            onward().start()

    def p_copy(k, j):
        low, size = extent(k)
        part = (pl.ds(j * tok, tok), pl.ds(low, size))
        return remote(
            sent.at[part], received.at[part], p_send.at[k, j], p_recv.at[k, j], (cross, twin)[j]
        )

    def out_copy(k):
        low, size = extent(k)
        return remote(
            pair_out.at[:, pl.ds(low, size)],
            out_ref.at[:, pl.ds(pl.multiple_of(mine + low, 128), size)],
            out_send.at[k],
            out_recv.at[k],
            core,
        )

    span_rows = LINE * rows
    last_start = pl.multiple_of(jnp.where(z < DEPTH // 2, (DEPTH - 1) * span_rows, 0), 128)
    first_start = pl.multiple_of(jnp.where(z < DEPTH // 2, 0, span_rows), 128)
    begun = [details[0] for name, *details in ORDER if name == "begin"]
    early = dict(zip(begun, sums))

    def product(slot, k, start=None, depth=None):
        if depth is None:
            left, right = attended[rows_of(slot), :], weights[k][...]
        else:
            inner_span = pl.ds(start, depth)
            left, right = attended[rows_of(slot), inner_span], weights[k][inner_span, :]
        return jnp.dot(left, right, preferred_element_type=jnp.float32)

    def far_part(j, k):
        if j == 0:
            arrive(k)
            if k not in early:
                owns[k].wait()
        low, size = extent(k)
        if k in early:
            part = early[k][pl.ds(j * tok, tok), :] + product(3 - j, k, last_start, span_rows)
        else:
            part = product(3 - j, k)
        sent[pl.ds(j * tok, tok), pl.ds(low, size)] = part.astype(jnp.bfloat16)
        p_copy(k, j).start()

    def begin(k):
        owns[k].wait()
        for j in range(2):
            part = product(3 - j, k, first_start, (DEPTH - 1) * span_rows)
            early[k][pl.ds(j * tok, tok), :] = part

    def blend(before, gate, part, flag):
        before = before.astype(jnp.float32)
        return jnp.where(flag > 0, before + gate * part, before).astype(jnp.bfloat16)

    def near_part(j, k):
        low, size = extent(k)
        cols = pl.ds(pl.multiple_of(mine + low, 128), size)
        local_cols = pl.ds(low, size)
        gate = gate_ref[:, cols]
        part = product(1 - j, k)
        for a in range(tiles):
            span = pl.ds(a * tile_rows, tile_rows)
            term = part[a * tile_rows : (a + 1) * tile_rows]
            if j == 0:
                pair_out[span, local_cols] = blend(
                    pair_in[span, local_cols], gate, term, flags[1][a]
                )
            else:
                out_ref[span, cols] = blend(mixed_in[span, cols], gate, term, flags[0][a])
        if j == 0:
            out_copy(k).start()

    def take(j, k):
        low, size = extent(k)
        p_copy(k, j).wait_recv()
        base = quarter_of(1 - y, b if j == 1 else 1 - b)
        cols = pl.ds(pl.multiple_of(base + low, 128), size)
        gate = gate_ref[:, cols]
        for a in range(tiles):
            span = pl.ds(a * tile_rows, tile_rows)
            part = received[pl.ds(j * tok + a * tile_rows, tile_rows), pl.ds(low, size)]
            out_ref[span, cols] = blend(
                mixed_in[span, cols], gate, part.astype(jnp.float32), flags[0][a]
            )

    def settle():
        for load in small:
            load.wait()
        for core_side in (b, 1 - b):
            flags.append([is_active(core_side, a) for a in range(tiles)])
        for a in range(tiles):
            use_near.append(is_listed(a, b * tiles + 1 - a))
            use_last.append(is_listed(a, (1 - b) * tiles + 1))
        for load in loads[:2]:
            load.wait()
        for g in range(sets):
            pl.loop(0, GROUPED // PACK)(functools.partial(split_pair, g))
            for copy in kv_swap(g):
                copy.start()
        loads[2].wait()
        for own in owns:
            own.start()
        for load in loads[3:]:
            load.start()
        swap_in.start()

    def collect():
        @pl.loop(0, pieces)
        def _(n):
            _, beside, onward = a_copies(n)
            beside().wait_recv()
            onward().wait_recv()

        for load in loads[3:]:
            load.wait()
        swap_in.wait_recv()
        pl.semaphore_wait(diagonal, 1)

    def drain_rest():
        swap_in.wait_send()
        for g in range(sets):
            for copy in kv_swap(g):
                copy.wait_send()

        @pl.loop(0, pieces)
        def _(n):
            for copy in a_copies(n):
                copy().wait_send()

    def drain(k):
        visit(k, 0, 0, done=True)
        if not z_first(k, 0):
            side(k, done=True)
        for u in (-1, 1, 2, 3):
            relay(k, u, done=True)

    share = pieces // sets
    steps = {
        "launch": launch,
        "settle": settle,
        "relay": relay,
        "side": side,
        "attend": attend_set,
        "forward": lambda g: pass_on(g * share, (g + 1) * share),
        "begin": begin,
        "far0": functools.partial(far_part, 0),
        "far1": functools.partial(far_part, 1),
        "near0": functools.partial(near_part, 0),
        "near1": functools.partial(near_part, 1),
        "take0": functools.partial(take, 0),
        "take1": functools.partial(take, 1),
        "drain": drain,
        "drain_rest": drain_rest,
    }
    collected = False
    for name, *details in ORDER:
        if name in ("begin", "far0") and not collected:
            collect()
            collected = True
        steps[name](*details)

    drained = [details[0] for name, *details in ORDER if name == "drain"]
    if ("drain_rest",) not in ORDER:
        drain_rest()
    for k in streams:
        if k not in drained:
            drain(k)
        for j in range(2):
            p_copy(k, j).wait_send()
        out_copy(k).wait()


def local_fused(
    count,
    block_input,
    gate,
    q_fresh,
    kv_fresh,
    kv_cache,
    active_list,
    active_count,
    key_list,
    out_weight,
):
    tok, width = block_input.shape
    rows = out_weight.shape[0]
    quarter = width // 4
    unit = quarter // UNITS
    columns = q_fresh.shape[1]
    heads = columns // HEAD_DIM
    sets = heads // GROUPED
    pieces = heads // PACK
    streams = len(STREAMS)
    anywhere = pl.BlockSpec(memory_space=pltpu.HBM)
    dma = pltpu.SemaphoreType.DMA

    def vmem(*shape):
        return pltpu.VMEM(shape, jnp.bfloat16)

    return pl.pallas_call(
        fused,
        out_shape=pltpu.VMEM((tok, width), jnp.bfloat16),
        in_specs=[anywhere] * 9,
        out_specs=pl.BlockSpec(memory_space=pltpu.VMEM),
        scratch_shapes=[
            [vmem(count * rows, size * unit) for _, size in STREAMS],
            vmem(tok, columns),
            vmem(tok, 2, columns),
            vmem(tok, 2, columns),
            pltpu.VMEM((PACK, 2 * tok, HEAD_DIM), jnp.float32),
            [vmem(2 * tok, GROUPED * HEAD_DIM) for _ in range(sets)],
            [vmem(2 * tok, GROUPED * HEAD_DIM) for _ in range(sets)],
            vmem(4 * tok, columns),
            vmem(tok, width),
            vmem(tok, quarter),
            vmem(tok, quarter),
            vmem(2 * tok, quarter),
            vmem(2 * tok, quarter),
            [
                pltpu.VMEM((2 * tok, STREAMS[details[0]][1] * unit), jnp.float32)
                for name, *details in ORDER
                if name == "begin"
            ],
            pltpu.VMEM((1, width), jnp.float32),
            pltpu.SMEM(active_list.shape, jnp.int32),
            pltpu.SMEM(active_count.shape, jnp.int32),
            pltpu.SMEM((key_list.shape[2],) + key_list.shape[:2], jnp.int32),
            dma((8,)),
            dma((streams,)),
            dma((streams, count, 3)),
            dma((streams, count)),
            dma((2, sets)),
            dma((2, sets)),
            dma((1,)),
            dma((1,)),
            dma((3, pieces)),
            dma((3, pieces)),
            dma((streams, 2)),
            dma((streams, 2)),
            dma((streams,)),
            dma((streams,)),
            pltpu.SemaphoreType.REGULAR,
        ],
        compiler_params=pltpu.CompilerParams(
            collective_id=0, has_side_effects=True, vmem_limit_bytes=56000000
        ),
    )(
        active_list,
        active_count,
        key_list.transpose(2, 0, 1),
        block_input,
        gate[None, :],
        q_fresh,
        kv_fresh,
        kv_cache,
        out_weight,
    )


def per_device(groups, count, cores, *args):
    rows, width = args[-1].shape
    columns = args[2].shape[1]
    fits = groups == 2 and cores == 2 and count == DEPTH * LINE and rows % 16 == 0
    fits = fits and width % (4 * UNITS * 128) == 0 and count * rows * width < 1 << 24
    fits = fits and columns % (GROUPED * HEAD_DIM) == 0 and LINE * rows % 128 == 0
    fits = fits and args[5].shape[2] == 2 and args[7].shape[1:] == (4, 3)
    return local_fused(count, *args) if fits else local(*args)


def solution(mesh):
    in_specs = (
        P(("groups", "fsdp", "blk"), None),
        P("groups"),
        P(("groups", "fsdp", "blk"), None),
        P(("groups", "fsdp", "blk"), None, None),
        P(("groups", "fsdp", "blk"), None, None),
        P(("groups", "fsdp"), None, None),
        P(("groups", "fsdp"), None),
        P(("groups", "fsdp"), None, None),
        P("fsdp", None),
    )
    sizes = [mesh.shape[axis] for axis in ("groups", "fsdp", "blk")]
    body = functools.partial(per_device, *sizes)
    out_specs = P(("groups", "fsdp", "blk"), None)
    return jax.shard_map(body, mesh=mesh, in_specs=in_specs, out_specs=out_specs, check_vma=False)
```
